32 devices in a mesh: gx: 4 (over z), gy: 8 (over y, x, core).
Axes of the slice: x: 2, y: 2, z: 4, core: 2. Of those that a mesh axis runs over, the one named last changes fastest.
Arguments:
- water_depth: float32 [256, 512], P('gy', 'gx'), may hold values from 0 to 2
- tracers: float32 [3, 256, 512], P(None, 'gy', 'gx'), may hold values from 0 to 2
- rainfall: float32 [256, 512], P('gy', 'gx'), may hold values from 0.2 to 1.5
- roughness: float32 [256, 512], P('gy', 'gx'), may hold values from 0.05 to 0.6
- flow_codes: int32 [256, 512], P('gy', 'gx'), may hold values from 0 to 7
- land_mask: int32 [256, 512], P('gy', 'gx'), may hold values 0 or 1
- leakance: float32 [64, 128], P('gy', 'gx'), may hold values from 0.05 to 2
- pumping: float32 [64, 128], P('gy', 'gx'), may hold values from -6 to 6
- active: int32 [64, 128], P('gy', 'gx'), may hold values 0 or 1
Outputs:
- depth_out: float32 [256, 512], P('gy', 'gx')
- tracers_out: float32 [3, 256, 512], P(None, 'gy', 'gx')
- head: float32 [64, 128], P('gy', 'gx')
The draws below stay inside these ranges and needn't reach their ends.
All inputs are finite; a program needn't handle non-finite values. No bound on the sum of `land_mask` or of `active` on one device may be relied on, other than what follows from the above.
Results may differ from the reference program's by a relative error of at most 0.0003.
Values sent between devices are 32-bit elements; how exact they have to be, the bound alone decides.
No kernel may reach another device: no remote copies, remote signals or barrier semaphores. Data moves between devices by JAX's collectives and lax.ppermute only.
A program may use at most 64 MiB of HBM per device.

```python
import math
import jax
import jax.numpy as jnp
from jax import lax

TRACERS = 3
SUBSTEPS = 12
ITERS = 2
NY = 256
NX = 512
NYC = 64
NXC = 128


def with_ends(drawn, rng, low, high):
    spot = [jax.random.randint(jax.random.fold_in(rng, axis), (), 0, length) for axis, length in enumerate(drawn.shape)]
    widest = drawn.shape.index(max(drawn.shape))
    beside = spot[:widest] + [(spot[widest] + 1) % drawn.shape[widest]] + spot[widest + 1:]
    return drawn.at[tuple(spot)].set(low).at[tuple(beside)].set(high)


def shard_levels(rng, extent, pieces, least, high):
    level = 1.0
    for position, parts in pieces:
        heights = jax.random.uniform(jax.random.fold_in(jax.random.fold_in(rng, 6), position), (parts,), jnp.float32, least / len(pieces), high / len(pieces))
        level = level * jnp.repeat(jnp.exp(heights), extent[position] // parts).reshape((-1,) + (1,) * (len(extent) - 1 - position))
    return level


def noise(key, dims, scale, reach, shards=(), held_as=jnp.bfloat16):
    factor_of = shard_levels(key, dims, shards, -0.22, 0.18) if shards else 1.0
    drawn = jax.random.normal(key, dims, jnp.float32) * scale * factor_of
    return jnp.minimum(jnp.maximum(drawn, -reach), reach).astype(held_as)


def setup_inputs(seed: int = 0) -> dict:
    key_list = jax.random.split(jax.random.key(seed), 10)
    return {
        "water_depth": jnp.clip(2.0 * jax.random.uniform(key_list[0], (NY, NX), jnp.float32) ** shard_levels(key_list[0], (NY, NX), ((0, 8), (1, 4)), -0.2, 0.2), 0.0, 2.0),
        "tracers": jnp.clip(2.0 * jax.random.uniform(key_list[1], (TRACERS, NY, NX), jnp.float32) ** shard_levels(key_list[1], (TRACERS, NY, NX), ((1, 8), (2, 4)), -0.2, 0.2), 0.0, 2.0),
        "rainfall": jnp.clip(0.2 + 1.3 * jax.random.uniform(key_list[2], (NY, NX), jnp.float32) ** shard_levels(key_list[2], (NY, NX), ((0, 8), (1, 4)), -0.2, 0.2), 0.2, 1.5),
        "roughness": jnp.clip(jnp.exp(math.log(0.6) - 2.4849067 * jax.random.uniform(key_list[3], (NY, NX), jnp.float32) ** shard_levels(key_list[3], (NY, NX), ((0, 8), (1, 4)), -0.2, 0.2)), 0.05, 0.6),
        "flow_codes": with_ends(jax.random.randint(key_list[4], (NY, NX), 0, 8), jax.random.fold_in(key_list[4], 1), 0, 7).astype(jnp.int32),
        "land_mask": with_ends((jax.random.randint(key_list[5], (NY, NX), 0, 8) < 7).astype(jnp.int32), jax.random.fold_in(key_list[5], 1), 0, 1),
        "leakance": jnp.clip(jnp.exp(math.log(2.0) - 3.6888794 * jax.random.uniform(key_list[6], (NYC, NXC), jnp.float32) ** shard_levels(key_list[6], (NYC, NXC), ((0, 8), (1, 4)), -0.2, 0.2)), 0.05, 2.0),
        "pumping": noise(key_list[7], (NYC, NXC), 1.0, 6.0, ((0, 8), (1, 4)), jnp.float32),
        "active": with_ends((jax.random.randint(key_list[8], (NYC, NXC), 0, 10) < 9).astype(jnp.int32), jax.random.fold_in(key_list[8], 1), 0, 1),
    }


TIME_STEP = 0.2
INFILTRATION = 0.05
NEIGHBOUR_MOVES = ((-1, -1), (-1, 0), (-1, 1), (0, -1), (0, 1), (1, -1), (1, 0), (1, 1))


def shift_into(field, drow, dcol):
    padded = jnp.pad(field, ((0, 0), (1, 1), (1, 1)))
    height = field.shape[1]
    breadth = field.shape[2]
    return lax.slice(padded, (0, 1 - drow, 1 - dcol), (field.shape[0], 1 - drow + height, 1 - dcol + breadth))


def overland_step(water_state, coef, flow_codes, land, rainfall):
    depth_now = water_state[0]
    rate = coef * jnp.cbrt(depth_now * depth_now)
    flux = rate[None] * water_state
    incoming = jnp.zeros_like(water_state)
    for heading in range(8):
        drow, dcol = NEIGHBOUR_MOVES[heading]
        leaving = jnp.where((flow_codes == heading)[None], flux, 0.0)
        incoming = incoming + shift_into(leaving, drow, dcol)
    source = jnp.concatenate([rainfall[None], jnp.zeros_like(water_state[1:])], axis=0)
    return land[None] * (water_state + TIME_STEP * (source - flux - INFILTRATION * water_state + incoming))


def aquifer_apply(field, actf, leakance):
    masked = jnp.pad(actf * field, 1)
    neighbours = masked[2:, 1:-1] + masked[:-2, 1:-1] + masked[1:-1, 2:] + masked[1:-1, :-2]
    return actf * ((4.0 + leakance) * field - neighbours) + (1.0 - actf) * field


def reference(water_depth, tracers, rainfall, roughness, flow_codes, land_mask, leakance, pumping, active):
    land = land_mask.astype(jnp.float32)
    coef = roughness * land
    water_state = jnp.concatenate([water_depth[None], tracers], axis=0) * land[None]

    def one_step(carried, ignored):
        state_now, recharge = carried
        recharge = recharge + INFILTRATION * TIME_STEP * state_now[0]
        state_now = overland_step(state_now, coef, flow_codes, land, rainfall)
        return (state_now, recharge), None

    (water_state, recharge), unused = lax.scan(one_step, (water_state, jnp.zeros_like(water_depth)), None, length=SUBSTEPS)
    coarse_rows = water_depth.shape[0] // 4
    coarse_cols = water_depth.shape[1] // 4
    recharge_coarse = recharge.reshape(coarse_rows, 4, coarse_cols, 4).sum(axis=(1, 3))
    actf = active.astype(jnp.float32)
    rhs = actf * (recharge_coarse - pumping)
    jacobi_diag = actf * (4.0 + leakance) + (1.0 - actf)
    head = jnp.zeros_like(rhs)
    resid = rhs
    precond = resid / jacobi_diag
    direction = precond
    weighted = jnp.sum(resid * precond)
    for sweep in range(ITERS):
        image = aquifer_apply(direction, actf, leakance)
        step_size = weighted / jnp.sum(direction * image)
        head = head + step_size * direction
        resid = resid - step_size * image
        if sweep + 1 < ITERS:
            precond = resid / jacobi_diag
            weighted_next = jnp.sum(resid * precond)
            direction = precond + (weighted_next / weighted) * direction
            weighted = weighted_next
    return water_state[0], water_state[1:], head
```

```python
import functools

import jax
import jax.numpy as jnp
from jax import lax
from jax.experimental import pallas as pl
from jax.experimental.pallas import tpu as pltpu
from jax.sharding import PartitionSpec as P

SUBSTEPS = 12
TIME_STEP = 0.2
INFILTRATION = 0.05
MOVES = ((-1, -1), (-1, 0), (-1, 1), (0, -1), (0, 1), (1, -1), (1, 0), (1, 1))
AXES = ("gx", "gy")

WIDE = 20
SLIM = 12
LANES = 128
SLOTS = ((0, WIDE), (WIDE, WIDE), (2 * WIDE, WIDE), (3 * WIDE, WIDE)) + tuple(
    (4 * WIDE + k * SLIM, SLIM) for k in range(3)
)
EAST_AT = 4 * WIDE + 3 * SLIM
WEST_AT = EAST_AT + WIDE
COARSE_AT = WEST_AT + WIDE
STRIP = 168
F32 = jnp.float32


def whole(count):
    return [pl.BlockSpec(memory_space=pltpu.VMEM)] * count


def lane_ids(rows):
    return lax.broadcasted_iota(jnp.int32, (rows, LANES), 1)


def pack_columns(depth, tracers, rain, rough, codes, land_mask, leak, pump, active, own, first, last, coarse):
    land = land_mask[...].astype(F32)
    fields = [
        depth[...] * land,
        rain[...] * land * TIME_STEP,
        rough[...] * land * TIME_STEP,
        codes[...].astype(F32),
        tracers[0] * land,
        tracers[1] * land,
        tracers[2] * land,
    ]
    rows = land.shape[0]
    ids = lane_ids(rows)
    head = jnp.zeros((rows, LANES), F32)
    tail = jnp.zeros((rows, LANES), F32)
    for field, (at, width) in zip(fields, SLOTS):
        spot = (ids >= at) & (ids < at + width)
        head = jnp.where(spot, pltpu.roll(field, at, 1) if at else field, head)
        tail = jnp.where(spot, pltpu.roll(field, (at + width) % LANES, 1), tail)
    for k, field in enumerate(fields):
        own[k] = field
    act = active[...].astype(F32)
    weight = act / (act * (4.0 + leak[...]) + (1.0 - act))
    both = jnp.concatenate([weight, pump[...], jnp.zeros((act.shape[0], LANES - 2 * act.shape[1]), F32)], axis=1)
    coarse[...] = both
    first[0:rows] = head
    last[0:rows] = tail
    first[rows : rows + act.shape[0]] = both
    last[rows : rows + act.shape[0]] = both


def pack_rows(own, east, west, coarse, first, last):
    rows = own.shape[1]
    crows = coarse.shape[0]
    for k, (at, width) in enumerate(SLOTS):
        first[at : at + width] = own[k, 0:width]
        last[at : at + width] = own[k, rows - width : rows]
    for at, side in ((EAST_AT, east), (WEST_AT, west)):
        first[at : at + WIDE] = side[0:WIDE]
        last[at : at + WIDE] = side[rows - WIDE : rows]
    for at, part in ((COARSE_AT, coarse), (COARSE_AT + 2, east.at[rows : rows + crows]), (COARSE_AT + 4, west.at[rows : rows + crows])):
        first[at : at + 2] = part[0:2]
        last[at : at + 2] = part[crows - 2 : crows]
    first[COARSE_AT + 6 : STRIP] = jnp.zeros((STRIP - COARSE_AT - 6, LANES), F32)
    last[COARSE_AT + 6 : STRIP] = jnp.zeros((STRIP - COARSE_AT - 6, LANES), F32)


def inside(counts):
    col = lax.axis_index("gx")
    row = lax.axis_index("gy")
    return row > 0, row < counts[1] - 1, col < counts[0] - 1, col > 0


def gather_fields(kinds, halo, own, east, west, north, south, flags, stage):
    has_north, has_south, has_east, has_west = flags
    rows = own.shape[1]
    total = rows + 2 * halo
    chunk = total // 8

    def lay(slot, at, width, middle):
        stage[slot, 0:halo] = jnp.where(has_north, north[at + width - halo : at + width], 0.0)
        stage[slot, halo : halo + rows] = middle
        stage[slot, halo + rows : total] = jnp.where(has_south, south[at : at + halo], 0.0)

    def read(slot):
        return [stage[slot, pl.ds(i, 8, stride=chunk)] for i in range(chunk)]

    for k in kinds:
        at, width = SLOTS[k]
        lay(k, at, width, own[k])
    lay(7, EAST_AT, WIDE, east[0:rows])
    lay(8, WEST_AT, WIDE, west[0:rows])
    east_parts = read(7)
    west_parts = read(8)
    ids = lane_ids(8)
    fields = []
    for k in kinds:
        at, width = SLOTS[k]
        in_east = ids < jnp.where(has_east, width, 0)
        in_west = ids >= jnp.where(has_west, LANES - width, LANES)
        parts = []
        for main, e, w in zip(read(k), east_parts, west_parts):
            e = pltpu.roll(e, (LANES - at) % LANES, 1) if at else e
            w = pltpu.roll(w, (2 * LANES - width - at) % LANES, 1)
            side = jnp.where(in_east, e, jnp.where(in_west, w, 0.0))
            parts.append(jnp.concatenate([main, side], axis=1)[None])
        fields.append(jnp.concatenate(parts, axis=0))
    return fields


def from_left(field):
    return pltpu.roll(field, 1, 2)


def from_right(field):
    return pltpu.roll(field, field.shape[2] - 1, 2)


def from_above(field):
    return jnp.concatenate([pltpu.roll(field[-1], 1, 0)[None], field[:-1]], axis=0)


def from_below(field):
    return jnp.concatenate([field[1:], pltpu.roll(field[0], 7, 0)[None]], axis=0)


def move_masks(codes, coef, masks):
    land = coef > 0.0
    sides = {-1: from_right(codes), 0: codes, 1: from_left(codes)}
    for k, (drow, dcol) in enumerate(MOVES):
        seen = sides[dcol]
        if drow == 1:
            seen = from_above(seen)
        elif drow == -1:
            seen = from_below(seen)
        masks[k] = jnp.where(land & (seen == float(k)), 1.0, 0.0)


def inflow(flux, masks):
    sides = {-1: from_right(flux), 0: flux, 1: from_left(flux)}
    total = None
    for dcol in (0, 1, -1):
        side = sides[dcol]
        for drow, seen in ((0, side), (1, from_above(side)), (-1, from_below(side))):
            if (drow, dcol) == (0, 0):
                continue
            term = masks[MOVES.index((drow, dcol))] * seen
            total = term if total is None else total + term
    return total


def speed(depth, coef):
    return coef * jnp.exp(jnp.log(jnp.abs(depth)) * (2.0 / 3.0))


KEEP = 1.0 - TIME_STEP * INFILTRATION


def depth_kernel(counts, own, east, west, north, south, coarse, sums, zc, uc, stage, masks, cst):
    flags = inside(counts)
    depth, rain, coef, codes = gather_fields((0, 1, 2, 3), WIDE, own, east, west, north, south, flags, stage)
    move_masks(codes, coef, masks)

    def step(_, carry):
        now, total = carry
        flux = speed(now, coef) * now
        return now * KEEP - flux + rain + inflow(flux, masks), total + now

    now, total = lax.fori_loop(0, SUBSTEPS - 1, step, (depth, jnp.zeros_like(depth)))
    total = total + now
    chunk = total.shape[0]
    for i in range(chunk):
        stage[0, pl.ds(i, 8, stride=chunk)] = total[i, :, :LANES]
        stage[1, pl.ds(i, 8, stride=chunk)] = total[i, :, LANES:]
    blocks = []
    for b in range(2):
        quads = [stage[b, pl.ds(8 + j, 16, stride=4)] for j in range(4)]
        blocks.append((quads[0] + quads[1]) + (quads[2] + quads[3]))
    pooled = jnp.concatenate(blocks, axis=1)
    crows, ccols = zc.shape[0], LANES // 4
    fine = lax.broadcasted_iota(jnp.int32, (2 * LANES, LANES), 0)
    cell = lax.broadcasted_iota(jnp.int32, (2 * LANES, LANES), 1)
    place = lax.shift_right_logical(fine, 2)
    near = fine < LANES + 8
    far = fine >= 2 * LANES - 8
    hit = (near & (place == cell)) | (far & (place - (2 * LANES // 4 - 2) == cell - (LANES - 2)))
    rc = jnp.dot(
        pooled,
        jnp.where(hit, 1.0, 0.0),
        precision=lax.Precision.HIGHEST,
        preferred_element_type=F32,
    ) * (INFILTRATION * TIME_STEP)

    has_north, has_south, has_east, has_west = flags
    rows = own.shape[1]
    for k, middle in enumerate((coarse[...], east[rows : rows + crows], west[rows : rows + crows])):
        at = COARSE_AT + 2 * k
        cst[k] = jnp.zeros((16, LANES), F32)
        cst[k, 1:3] = jnp.where(has_north, north[at : at + 2], 0.0)
        cst[k, 3 : 3 + crows] = middle
        cst[k, 3 + crows : 5 + crows] = jnp.where(has_south, south[at : at + 2], 0.0)
    ids = lane_ids(16)
    e_here = (ids >= ccols) & (ids < jnp.where(has_east, ccols + 2, ccols))
    w_here = ids >= jnp.where(has_west, LANES - 2, LANES)
    pair = []
    for shift in (0, ccols):
        main = pltpu.roll(cst[0], LANES - shift, 1) if shift else cst[0]
        e = pltpu.roll(cst[1], (LANES + ccols - shift) % LANES, 1) if shift != ccols else cst[1]
        w = pltpu.roll(cst[2], (2 * LANES - ccols - shift) % LANES, 1)
        pair.append(jnp.where(ids < ccols, main, jnp.where(e_here, e, jnp.where(w_here, w, 0.0))))
    weight, pump = pair

    def beside(v):
        return (pltpu.roll(v, 1, 1) + pltpu.roll(v, LANES - 1, 1)) + (pltpu.roll(v, 1, 0) + pltpu.roll(v, 15, 0))

    drive = rc - pump
    z = weight * drive
    nz = beside(z)
    u = weight * nz
    nu = beside(u)
    mine = (ids < ccols)[3 : 3 + crows]
    cut = lambda v: v[3 : 3 + crows]
    z, nz, u, nu, drive = cut(z), cut(nz), cut(u), cut(nu), cut(drive)
    z = jnp.where(mine, z, 0.0)
    u = jnp.where(mine, u, 0.0)
    lines = [jnp.sum(a * b, axis=0, keepdims=True) for a, b in ((drive, z), (z, nz), (u, nz), (u, nu))]
    sums[...] = jnp.concatenate(lines + [jnp.zeros((4, LANES), F32)], axis=0)
    zc[...] = z
    uc[...] = u


def state_kernel(counts, own, east, west, north, south, depth_out, tracers_out, stage, masks):
    flags = inside(counts)
    depth, rain, coef, codes, *species = gather_fields(
        (0, 1, 2, 3, 4, 5, 6), SLIM, own, east, west, north, south, flags, stage
    )
    move_masks(codes, coef, masks)

    def step(_, carry):
        now = carry[0]
        rate = speed(now, coef)
        flux = rate * now
        new = [now * KEEP - flux + rain + inflow(flux, masks)]
        for held in carry[1:]:
            flux = rate * held
            new.append(held * KEEP - flux + inflow(flux, masks))
        return tuple(new)

    final = lax.fori_loop(0, SUBSTEPS, step, (depth, *species))
    chunk = depth.shape[0]
    rows = own.shape[1]
    for k, field in enumerate(final):
        for i in range(chunk):
            stage[k, pl.ds(i, 8, stride=chunk)] = field[i, :, :LANES]
        if k == 0:
            depth_out[...] = stage[k, SLIM : SLIM + rows]
        else:
            tracers_out[k - 1] = stage[k, SLIM : SLIM + rows]


def head_kernel(sums, zc, uc, head):
    n = jnp.sum(sums[...], axis=1, keepdims=True)
    n0, n1, n2, n3 = n[0:1], n[1:2], n[2:3], n[3:4]
    pq = n0 - n1
    a0 = n0 / pq
    ratio = (n0 * n2 - n1 * n1) / (pq * pq)
    slope = (n1 - n2) / pq
    below = (n2 - n3) - slope * (n1 - n2)
    a1 = jnp.where(below > 0.0, n0 * ratio / jnp.where(below > 0.0, below, 1.0), 0.0) / a0
    wide = head.shape[1]
    head[...] = ((a0 - a1 * slope) * zc[...] + a1 * uc[...])[:, :wide]


def ring(shift, axis, counts):
    size = counts[AXES.index(axis)]
    return [(i, (i + shift) % size) for i in range(size)]


def exchange(first, last, axis, counts):
    after = lax.ppermute(first, axis, ring(-1, axis, counts))
    before = lax.ppermute(last, axis, ring(1, axis, counts))
    return after, before


def everywhere(value, counts):
    size = counts[0] * counts[1]
    if size & (size - 1):
        return lax.psum(value, AXES)
    bit = 1
    while bit < size:
        value = value + lax.ppermute(value, AXES, [(i, i ^ bit) for i in range(size)])
        bit *= 2
    return value


def shards(counts, water_depth, tracers, rainfall, roughness, flow_codes, land_mask, leakance, pumping, active):
    rows, cols = water_depth.shape
    crows, ccols = leakance.shape
    shape = lambda *dims: jax.ShapeDtypeStruct(dims, F32)
    own, first, last, coarse = pl.pallas_call(
        pack_columns,
        out_shape=(shape(7, rows, cols), shape(rows + crows, LANES), shape(rows + crows, LANES), shape(crows, LANES)),
        in_specs=whole(9),
        out_specs=tuple(whole(4)),
        name="pack_columns",
    )(water_depth, tracers, rainfall, roughness, flow_codes, land_mask, leakance, pumping, active)
    east, west = exchange(first, last, "gx", counts)
    first, last = pl.pallas_call(
        pack_rows,
        out_shape=(shape(STRIP, LANES), shape(STRIP, LANES)),
        in_specs=whole(4),
        out_specs=tuple(whole(2)),
        name="pack_rows",
    )(own, east, west, coarse)
    south, north = exchange(first, last, "gy", counts)
    deep = rows + 2 * WIDE
    sums, zc, uc = pl.pallas_call(
        functools.partial(depth_kernel, counts),
        out_shape=(shape(8, LANES), shape(crows, LANES), shape(crows, LANES)),
        in_specs=whole(6),
        out_specs=tuple(whole(3)),
        scratch_shapes=[
            pltpu.VMEM((9, deep, LANES), F32),
            pltpu.VMEM((8, deep // 8, 8, 2 * LANES), F32),
            pltpu.VMEM((3, 16, LANES), F32),
        ],
        name="depth_and_moments",
    )(own, east, west, north, south, coarse)
    low = rows + 2 * SLIM
    depth_out, tracers_out = pl.pallas_call(
        functools.partial(state_kernel, counts),
        out_shape=(shape(rows, cols), shape(3, rows, cols)),
        in_specs=whole(5),
        out_specs=tuple(whole(2)),
        scratch_shapes=[
            pltpu.VMEM((9, low, LANES), F32),
            pltpu.VMEM((8, low // 8, 8, 2 * LANES), F32),
        ],
        cost_estimate=pl.CostEstimate(flops=20_000_000, bytes_accessed=20_000_000, transcendentals=0),
        name="all_channels",
    )(own, east, west, north, south)
    sums = everywhere(sums, counts)
    head = pl.pallas_call(
        head_kernel,
        out_shape=shape(crows, ccols),
        in_specs=whole(3),
        out_specs=pl.BlockSpec(memory_space=pltpu.VMEM),
        name="combine_head",
    )(sums, zc, uc)
    return depth_out, tracers_out, head


def solution(mesh):
    counts = (mesh.shape["gx"], mesh.shape["gy"])
    tile = P("gy", "gx")
    deep = P(None, "gy", "gx")
    return jax.shard_map(
        functools.partial(shards, counts),
        mesh=mesh,
        in_specs=(tile, deep) + (tile,) * 7,
        out_specs=(tile, deep, tile),
        check_vma=False,
    )
```

```python
import functools

import jax
import jax.numpy as jnp
from jax import lax
from jax.experimental import pallas as pl
from jax.experimental.pallas import tpu as pltpu
from jax.sharding import PartitionSpec as P

SUBSTEPS = 12
TIME_STEP = 0.2
INFILTRATION = 0.05
MOVES = ((-1, -1), (-1, 0), (-1, 1), (0, -1), (0, 1), (1, -1), (1, 0), (1, 1))
AXES = ("gx", "gy")

WIDE = 20
SLIM = 12
LANES = 128
SLOTS = ((0, WIDE), (WIDE, WIDE), (2 * WIDE, WIDE), (3 * WIDE, WIDE)) + tuple(
    (4 * WIDE + k * SLIM, SLIM) for k in range(3)
)
EAST_AT = 4 * WIDE + 3 * SLIM
WEST_AT = EAST_AT + WIDE
COARSE_AT = WEST_AT + WIDE
STRIP = 168
F32 = jnp.float32
SMALL = pltpu.CompilerParams(vmem_limit_bytes=2 << 20)
ROOMY = pltpu.CompilerParams(vmem_limit_bytes=6 << 20)


def whole(count):
    return [pl.BlockSpec(memory_space=pltpu.VMEM)] * count


def lane_ids(rows):
    return lax.broadcasted_iota(jnp.int32, (rows, LANES), 1)


def pack_columns(*refs):
    sources, (own, first, last, coarse), buffers, done = refs[:9], refs[9:13], refs[13:22], refs[22]
    copies = [pltpu.make_async_copy(a, b, done.at[k]) for k, (a, b) in enumerate(zip(sources, buffers))]
    for copy in copies:
        copy.start()
    for copy in copies:
        copy.wait()
    depth, tracers, rain, rough, codes, land_mask, leak, pump, active = buffers
    land = land_mask[...].astype(F32)
    fields = [
        depth[...] * land,
        rain[...] * land * TIME_STEP,
        rough[...] * land * TIME_STEP,
        codes[...].astype(F32),
        tracers[0] * land,
        tracers[1] * land,
        tracers[2] * land,
    ]
    rows = land.shape[0]
    ids = lane_ids(rows)
    head = jnp.zeros((rows, LANES), F32)
    tail = jnp.zeros((rows, LANES), F32)
    for field, (at, width) in zip(fields, SLOTS):
        spot = (ids >= at) & (ids < at + width)
        head = jnp.where(spot, pltpu.roll(field, at, 1) if at else field, head)
        tail = jnp.where(spot, pltpu.roll(field, (at + width) % LANES, 1), tail)
    for k, field in enumerate(fields):
        own[k] = field
    act = active[...].astype(F32)
    weight = act / (act * (4.0 + leak[...]) + (1.0 - act))
    both = jnp.concatenate([weight, pump[...], jnp.zeros((act.shape[0], LANES - 2 * act.shape[1]), F32)], axis=1)
    coarse[...] = both
    first[0:rows] = head
    last[0:rows] = tail
    first[rows : rows + act.shape[0]] = both
    last[rows : rows + act.shape[0]] = both


def pack_rows(own, east, west, coarse, first, last):
    rows = own.shape[1]
    crows = coarse.shape[0]
    for k, (at, width) in enumerate(SLOTS):
        first[at : at + width] = own[k, 0:width]
        last[at : at + width] = own[k, rows - width : rows]
    for at, side in ((EAST_AT, east), (WEST_AT, west)):
        first[at : at + WIDE] = side[0:WIDE]
        last[at : at + WIDE] = side[rows - WIDE : rows]
    for at, part in ((COARSE_AT, coarse), (COARSE_AT + 2, east.at[rows : rows + crows]), (COARSE_AT + 4, west.at[rows : rows + crows])):
        first[at : at + 2] = part[0:2]
        last[at : at + 2] = part[crows - 2 : crows]
    first[COARSE_AT + 6 : STRIP] = jnp.zeros((STRIP - COARSE_AT - 6, LANES), F32)
    last[COARSE_AT + 6 : STRIP] = jnp.zeros((STRIP - COARSE_AT - 6, LANES), F32)


def inside(counts):
    col = lax.axis_index("gx")
    row = lax.axis_index("gy")
    return row > 0, row < counts[1] - 1, col < counts[0] - 1, col > 0


def gather_fields(kinds, halo, own, east, west, north, south, flags, stage):
    has_north, has_south, has_east, has_west = flags
    rows = own.shape[1]
    total = rows + 2 * halo
    chunk = total // 8

    def lay(slot, at, width, middle):
        stage[slot, 0:halo] = jnp.where(has_north, north[at + width - halo : at + width], 0.0)
        stage[slot, halo : halo + rows] = middle
        stage[slot, halo + rows : total] = jnp.where(has_south, south[at : at + halo], 0.0)

    def read(slot):
        return [stage[slot, pl.ds(i, 8, stride=chunk)] for i in range(chunk)]

    for k in kinds:
        at, width = SLOTS[k]
        lay(k, at, width, own[k])
    lay(7, EAST_AT, WIDE, east[0:rows])
    lay(8, WEST_AT, WIDE, west[0:rows])
    east_parts = read(7)
    west_parts = read(8)
    ids = lane_ids(8)
    fields = []
    for k in kinds:
        at, width = SLOTS[k]
        in_east = ids < jnp.where(has_east, width, 0)
        in_west = ids >= jnp.where(has_west, LANES - width, LANES)
        parts = []
        for main, e, w in zip(read(k), east_parts, west_parts):
            e = pltpu.roll(e, (LANES - at) % LANES, 1) if at else e
            w = pltpu.roll(w, (2 * LANES - width - at) % LANES, 1)
            side = jnp.where(in_east, e, jnp.where(in_west, w, 0.0))
            parts.append(jnp.concatenate([main, side], axis=1)[None])
        fields.append(jnp.concatenate(parts, axis=0))
    return fields


def from_left(field):
    return pltpu.roll(field, 1, 2)


def from_right(field):
    return pltpu.roll(field, field.shape[2] - 1, 2)


def from_above(field):
    return jnp.concatenate([pltpu.roll(field[-1], 1, 0)[None], field[:-1]], axis=0)


def from_below(field):
    return jnp.concatenate([field[1:], pltpu.roll(field[0], 7, 0)[None]], axis=0)


def move_masks(codes, coef, masks):
    land = coef > 0.0
    sides = {-1: from_right(codes), 0: codes, 1: from_left(codes)}
    for k, (drow, dcol) in enumerate(MOVES):
        seen = sides[dcol]
        if drow == 1:
            seen = from_above(seen)
        elif drow == -1:
            seen = from_below(seen)
        masks[k] = jnp.where(land & (seen == float(k)), 1.0, 0.0)


def inflow(flux, masks):
    sides = {-1: from_right(flux), 0: flux, 1: from_left(flux)}
    total = None
    for dcol in (0, 1, -1):
        side = sides[dcol]
        for drow, seen in ((0, side), (1, from_above(side)), (-1, from_below(side))):
            if (drow, dcol) == (0, 0):
                continue
            term = masks[MOVES.index((drow, dcol))] * seen
            total = term if total is None else total + term
    return total


def speed(depth, coef):
    return coef * jnp.exp(jnp.log(jnp.abs(depth)) * (2.0 / 3.0))


KEEP = 1.0 - TIME_STEP * INFILTRATION


def depth_kernel(counts, own, east, west, north, south, coarse, sums, zc, uc, stage, masks, cst):
    flags = inside(counts)
    depth, rain, coef, codes = gather_fields((0, 1, 2, 3), WIDE, own, east, west, north, south, flags, stage)
    move_masks(codes, coef, masks)

    def step(_, carry):
        now, total = carry
        flux = speed(now, coef) * now
        return now * KEEP - flux + rain + inflow(flux, masks), total + now

    now, total = lax.fori_loop(0, SUBSTEPS - 1, step, (depth, jnp.zeros_like(depth)))
    total = total + now
    chunk = total.shape[0]
    for i in range(chunk):
        stage[0, pl.ds(i, 8, stride=chunk)] = total[i, :, :LANES]
        stage[1, pl.ds(i, 8, stride=chunk)] = total[i, :, LANES:]
    blocks = []
    for b in range(2):
        quads = [stage[b, pl.ds(8 + j, 16, stride=4)] for j in range(4)]
        blocks.append((quads[0] + quads[1]) + (quads[2] + quads[3]))
    pooled = jnp.concatenate(blocks, axis=1)
    crows, ccols = zc.shape[0], LANES // 4
    fine = lax.broadcasted_iota(jnp.int32, (2 * LANES, LANES), 0)
    cell = lax.broadcasted_iota(jnp.int32, (2 * LANES, LANES), 1)
    place = lax.shift_right_logical(fine, 2)
    near = fine < LANES + 8
    far = fine >= 2 * LANES - 8
    hit = (near & (place == cell)) | (far & (place - (2 * LANES // 4 - 2) == cell - (LANES - 2)))
    rc = jnp.dot(
        pooled,
        jnp.where(hit, 1.0, 0.0),
        precision=lax.Precision.HIGHEST,
        preferred_element_type=F32,
    ) * (INFILTRATION * TIME_STEP)

    has_north, has_south, has_east, has_west = flags
    rows = own.shape[1]
    for k, middle in enumerate((coarse[...], east[rows : rows + crows], west[rows : rows + crows])):
        at = COARSE_AT + 2 * k
        cst[k] = jnp.zeros((16, LANES), F32)
        cst[k, 1:3] = jnp.where(has_north, north[at : at + 2], 0.0)
        cst[k, 3 : 3 + crows] = middle
        cst[k, 3 + crows : 5 + crows] = jnp.where(has_south, south[at : at + 2], 0.0)
    ids = lane_ids(16)
    e_here = (ids >= ccols) & (ids < jnp.where(has_east, ccols + 2, ccols))
    w_here = ids >= jnp.where(has_west, LANES - 2, LANES)
    pair = []
    for shift in (0, ccols):
        main = pltpu.roll(cst[0], LANES - shift, 1) if shift else cst[0]
        e = pltpu.roll(cst[1], (LANES + ccols - shift) % LANES, 1) if shift != ccols else cst[1]
        w = pltpu.roll(cst[2], (2 * LANES - ccols - shift) % LANES, 1)
        pair.append(jnp.where(ids < ccols, main, jnp.where(e_here, e, jnp.where(w_here, w, 0.0))))
    weight, pump = pair

    def beside(v):
        return (pltpu.roll(v, 1, 1) + pltpu.roll(v, LANES - 1, 1)) + (pltpu.roll(v, 1, 0) + pltpu.roll(v, 15, 0))

    drive = rc - pump
    z = weight * drive
    nz = beside(z)
    u = weight * nz
    nu = beside(u)
    mine = (ids < ccols)[3 : 3 + crows]
    cut = lambda v: v[3 : 3 + crows]
    z, nz, u, nu, drive = cut(z), cut(nz), cut(u), cut(nu), cut(drive)
    z = jnp.where(mine, z, 0.0)
    u = jnp.where(mine, u, 0.0)
    row = jnp.zeros((crows, LANES), F32)
    for k, (a, b) in enumerate(((drive, z), (z, nz), (u, nz), (u, nu))):
        part = a * b
        row = row + (pltpu.roll(part, k * ccols, 1) if k else part)
    row = jnp.sum(row, axis=0, keepdims=True)
    sums[...] = jnp.broadcast_to(row, sums.shape)
    zc[...] = z
    uc[...] = u


def state_kernel(counts, own, east, west, north, south, depth_out, tracers_out, stage, masks):
    flags = inside(counts)
    depth, rain, coef, codes, *species = gather_fields(
        (0, 1, 2, 3, 4, 5, 6), SLIM, own, east, west, north, south, flags, stage
    )
    move_masks(codes, coef, masks)

    def step(_, carry):
        now = carry[0]
        rate = speed(now, coef)
        flux = rate * now
        new = [now * KEEP - flux + rain + inflow(flux, masks)]
        for held in carry[1:]:
            flux = rate * held
            new.append(held * KEEP - flux + inflow(flux, masks))
        return tuple(new)

    final = lax.fori_loop(0, SUBSTEPS, step, (depth, *species))
    chunk = depth.shape[0]
    rows = own.shape[1]
    for k, field in enumerate(final):
        for i in range(chunk):
            stage[k, pl.ds(i, 8, stride=chunk)] = field[i, :, :LANES]
        if k == 0:
            depth_out[...] = stage[k, SLIM : SLIM + rows]
        else:
            tracers_out[k - 1] = stage[k, SLIM : SLIM + rows]


def head_kernel(sums, zc, uc, head):
    total = jnp.sum(sums[...], axis=0, keepdims=True)
    run = LANES // 4
    ids = lane_ids(1)
    n0, n1, n2, n3 = (
        jnp.sum(jnp.where((ids >= k * run) & (ids < (k + 1) * run), total, 0.0), axis=1, keepdims=True)
        for k in range(4)
    )
    pq = n0 - n1
    a0 = n0 / pq
    ratio = (n0 * n2 - n1 * n1) / (pq * pq)
    slope = (n1 - n2) / pq
    below = (n2 - n3) - slope * (n1 - n2)
    a1 = jnp.where(below > 0.0, n0 * ratio / jnp.where(below > 0.0, below, 1.0), 0.0) / a0
    wide = head.shape[1]
    head[...] = ((a0 - a1 * slope) * zc[...] + a1 * uc[...])[:, :wide]


def ring(shift, axis, counts):
    size = counts[AXES.index(axis)]
    return [(i, (i + shift) % size) for i in range(size)]


def exchange(first, last, axis, counts):
    after = lax.ppermute(first, axis, ring(-1, axis, counts))
    before = lax.ppermute(last, axis, ring(1, axis, counts))
    return after, before


def shards(counts, *inputs):
    rows, cols = inputs[0].shape
    crows, ccols = inputs[6].shape
    shape = lambda *dims: jax.ShapeDtypeStruct(dims, F32)
    own, first, last, coarse = pl.pallas_call(
        pack_columns,
        out_shape=(shape(7, rows, cols), shape(rows + crows, LANES), shape(rows + crows, LANES), shape(crows, LANES)),
        in_specs=[pl.BlockSpec(memory_space=pltpu.MemorySpace.HBM)] * 9,
        out_specs=tuple(whole(4)),
        scratch_shapes=[pltpu.VMEM(a.shape, a.dtype) for a in inputs] + [pltpu.SemaphoreType.DMA((9,))],
        compiler_params=SMALL,
        name="pack_columns",
    )(*[pltpu.with_memory_space_constraint(a, pltpu.MemorySpace.HBM) for a in inputs])
    east, west = exchange(first, last, "gx", counts)
    first, last = pl.pallas_call(
        pack_rows,
        out_shape=(shape(STRIP, LANES), shape(STRIP, LANES)),
        in_specs=whole(4),
        out_specs=tuple(whole(2)),
        compiler_params=SMALL,
        name="pack_rows",
    )(own, east, west, coarse)
    south, north = exchange(first, last, "gy", counts)
    deep = rows + 2 * WIDE
    sums, zc, uc = pl.pallas_call(
        functools.partial(depth_kernel, counts),
        out_shape=(shape(counts[0] * counts[1], LANES), shape(crows, LANES), shape(crows, LANES)),
        in_specs=whole(6),
        out_specs=tuple(whole(3)),
        scratch_shapes=[
            pltpu.VMEM((9, deep, LANES), F32),
            pltpu.VMEM((8, deep // 8, 8, 2 * LANES), F32),
            pltpu.VMEM((3, 16, LANES), F32),
        ],
        compiler_params=ROOMY,
        name="depth_and_moments",
    )(own, east, west, north, south, coarse)
    low = rows + 2 * SLIM
    depth_out, tracers_out = pl.pallas_call(
        functools.partial(state_kernel, counts),
        out_shape=(shape(rows, cols), shape(3, rows, cols)),
        in_specs=whole(5),
        out_specs=tuple(whole(2)),
        scratch_shapes=[
            pltpu.VMEM((9, low, LANES), F32),
            pltpu.VMEM((8, low // 8, 8, 2 * LANES), F32),
        ],
        cost_estimate=pl.CostEstimate(flops=20_000_000, bytes_accessed=20_000_000, transcendentals=0),
        compiler_params=ROOMY,
        name="all_channels",
    )(own, east, west, north, south)
    sums = lax.all_to_all(sums, AXES, 0, 0, tiled=True)
    head = pl.pallas_call(
        head_kernel,
        out_shape=shape(crows, ccols),
        in_specs=whole(3),
        out_specs=pl.BlockSpec(memory_space=pltpu.VMEM),
        compiler_params=SMALL,
        name="combine_head",
    )(sums, zc, uc)
    return depth_out, tracers_out, head


def solution(mesh):
    counts = (mesh.shape["gx"], mesh.shape["gy"])
    tile = P("gy", "gx")
    deep = P(None, "gy", "gx")
    return jax.shard_map(
        functools.partial(shards, counts),
        mesh=mesh,
        in_specs=(tile, deep) + (tile,) * 7,
        out_specs=(tile, deep, tile),
        check_vma=False,
    )
```

```python
import functools

import jax
import jax.numpy as jnp
from jax import lax
from jax.experimental import pallas as pl
from jax.experimental.pallas import tpu as pltpu
from jax.sharding import PartitionSpec as P

SUBSTEPS = 12
TIME_STEP = 0.2
INFILTRATION = 0.05
MOVES = ((-1, -1), (-1, 0), (-1, 1), (0, -1), (0, 1), (1, -1), (1, 0), (1, 1))
AXES = ("gx", "gy")

WIDE = 20
SLIM = 12
LANES = 128
SLOTS = ((0, WIDE), (WIDE, WIDE), (2 * WIDE, WIDE), (3 * WIDE, WIDE)) + tuple(
    (4 * WIDE + k * SLIM, SLIM) for k in range(3)
)
EAST_AT = 4 * WIDE + 3 * SLIM
WEST_AT = EAST_AT + WIDE
COARSE_AT = WEST_AT + WIDE
STRIP = 168
F32 = jnp.float32
SMALL = pltpu.CompilerParams(vmem_limit_bytes=2 << 20)
ROOMY = pltpu.CompilerParams(vmem_limit_bytes=6 << 20)


def whole(count):
    return [pl.BlockSpec(memory_space=pltpu.VMEM)] * count


def lane_ids(rows):
    return lax.broadcasted_iota(jnp.int32, (rows, LANES), 1)


def pack_columns(*refs):
    sources, (own, near, far, coarse), buffers, done = refs[:9], refs[9:13], refs[13:22], refs[22]
    copies = [pltpu.make_async_copy(a, b, done.at[k]) for k, (a, b) in enumerate(zip(sources, buffers))]
    for copy in copies:
        copy.start()
    for copy in copies:
        copy.wait()
    depth, tracers, rain, rough, codes, land_mask, leak, pump, active = buffers
    land = land_mask[...].astype(F32)
    fields = [
        depth[...] * land,
        rain[...] * land * TIME_STEP,
        rough[...] * land * TIME_STEP,
        codes[...].astype(F32),
        tracers[0] * land,
        tracers[1] * land,
        tracers[2] * land,
    ]
    rows = land.shape[0]
    ids = lane_ids(rows)
    head = jnp.zeros((rows, LANES), F32)
    tail = jnp.zeros((rows, LANES), F32)
    for field, (at, width) in zip(fields, SLOTS):
        spot = (ids >= at) & (ids < at + width)
        head = jnp.where(spot, pltpu.roll(field, at, 1) if at else field, head)
        tail = jnp.where(spot, pltpu.roll(field, (at + width) % LANES, 1), tail)
    for k, field in enumerate(fields):
        own[k] = field
    act = active[...].astype(F32)
    weight = act / (act * (4.0 + leak[...]) + (1.0 - act))
    both = jnp.concatenate([weight, pump[...], jnp.zeros((act.shape[0], LANES - 2 * act.shape[1]), F32)], axis=1)
    coarse[...] = both
    odd = lax.axis_index("gx") % 2 == 1
    near[0:rows] = jnp.where(odd, head, tail)
    far[0:rows] = jnp.where(odd, tail, head)
    near[rows : rows + act.shape[0]] = both
    far[rows : rows + act.shape[0]] = both


def pack_rows(own, side_near, side_far, coarse, near, far, east, west):
    flip = lax.axis_index("gx") % 2 == 1
    east[...] = jnp.where(flip, side_far[...], side_near[...])
    west[...] = jnp.where(flip, side_near[...], side_far[...])
    rows = own.shape[1]
    crows = coarse.shape[0]
    odd = lax.axis_index("gy") % 2 == 1

    def put(at, top, bottom):
        near[at : at + top.shape[0]] = jnp.where(odd, top, bottom)
        far[at : at + top.shape[0]] = jnp.where(odd, bottom, top)

    for k, (at, width) in enumerate(SLOTS):
        put(at, own[k, 0:width], own[k, rows - width : rows])
    for at, side in ((EAST_AT, east), (WEST_AT, west)):
        put(at, side[0:WIDE], side[rows - WIDE : rows])
    for at, part in ((COARSE_AT, coarse), (COARSE_AT + 2, east.at[rows : rows + crows]), (COARSE_AT + 4, west.at[rows : rows + crows])):
        put(at, part[0:2], part[crows - 2 : crows])
    rest = jnp.zeros((STRIP - COARSE_AT - 6, LANES), F32)
    near[COARSE_AT + 6 : STRIP] = rest
    far[COARSE_AT + 6 : STRIP] = rest


def inside(counts):
    col = lax.axis_index("gx")
    row = lax.axis_index("gy")
    return row > 0, row < counts[1] - 1, col < counts[0] - 1, col > 0


def rows_from(near, far, start, count, use_near, present):
    got = jnp.where(use_near, near[start : start + count], far[start : start + count])
    return jnp.where(present, got, 0.0)


def gather_fields(kinds, halo, own, east, west, near, far, flags, stage):
    has_north, has_south, has_east, has_west = flags
    rows = own.shape[1]
    total = rows + 2 * halo
    chunk = total // 8
    odd = lax.axis_index("gy") % 2 == 1

    def lay(slot, at, width, middle):
        stage[slot, 0:halo] = rows_from(near, far, at + width - halo, halo, odd, has_north)
        stage[slot, halo : halo + rows] = middle
        stage[slot, halo + rows : total] = rows_from(near, far, at, halo, ~odd, has_south)

    def read(slot):
        return [stage[slot, pl.ds(i, 8, stride=chunk)] for i in range(chunk)]

    for k in kinds:
        at, width = SLOTS[k]
        lay(k, at, width, own[k])
    lay(7, EAST_AT, WIDE, east[0:rows])
    lay(8, WEST_AT, WIDE, west[0:rows])
    east_parts = read(7)
    west_parts = read(8)
    ids = lane_ids(8)
    fields = []
    for k in kinds:
        at, width = SLOTS[k]
        in_east = ids < jnp.where(has_east, width, 0)
        in_west = ids >= jnp.where(has_west, LANES - width, LANES)
        parts = []
        for main, e, w in zip(read(k), east_parts, west_parts):
            e = pltpu.roll(e, (LANES - at) % LANES, 1) if at else e
            w = pltpu.roll(w, (2 * LANES - width - at) % LANES, 1)
            side = jnp.where(in_east, e, jnp.where(in_west, w, 0.0))
            parts.append(jnp.concatenate([main, side], axis=1)[None])
        fields.append(jnp.concatenate(parts, axis=0))
    return fields


def from_left(field):
    return pltpu.roll(field, 1, 2)


def from_right(field):
    return pltpu.roll(field, field.shape[2] - 1, 2)


def from_above(field):
    return jnp.concatenate([pltpu.roll(field[-1], 1, 0)[None], field[:-1]], axis=0)


def from_below(field):
    return jnp.concatenate([field[1:], pltpu.roll(field[0], 7, 0)[None]], axis=0)


def move_masks(codes, coef, masks):
    land = coef > 0.0
    sides = {-1: from_right(codes), 0: codes, 1: from_left(codes)}
    for k, (drow, dcol) in enumerate(MOVES):
        seen = sides[dcol]
        if drow == 1:
            seen = from_above(seen)
        elif drow == -1:
            seen = from_below(seen)
        masks[k] = jnp.where(land & (seen == float(k)), 1.0, 0.0)


def inflow(flux, masks):
    sides = {-1: from_right(flux), 0: flux, 1: from_left(flux)}
    total = None
    for dcol in (0, 1, -1):
        side = sides[dcol]
        for drow, seen in ((0, side), (1, from_above(side)), (-1, from_below(side))):
            if (drow, dcol) == (0, 0):
                continue
            term = masks[MOVES.index((drow, dcol))] * seen
            total = term if total is None else total + term
    return total


def speed(depth, coef):
    return coef * jnp.exp(jnp.log(jnp.abs(depth)) * (2.0 / 3.0))


KEEP = 1.0 - TIME_STEP * INFILTRATION


def depth_kernel(counts, own, east, west, near, far, coarse, sums, zc, uc, stage, masks, cst):
    flags = inside(counts)
    depth, rain, coef, codes = gather_fields((0, 1, 2, 3), WIDE, own, east, west, near, far, flags, stage)
    move_masks(codes, coef, masks)

    def step(_, carry):
        now, total = carry
        flux = speed(now, coef) * now
        return now * KEEP - flux + rain + inflow(flux, masks), total + now

    now, total = lax.fori_loop(0, SUBSTEPS - 1, step, (depth, jnp.zeros_like(depth)))
    total = total + now
    chunk = total.shape[0]
    for i in range(chunk):
        stage[0, pl.ds(i, 8, stride=chunk)] = total[i, :, :LANES]
        stage[1, pl.ds(i, 8, stride=chunk)] = total[i, :, LANES:]
    blocks = []
    for b in range(2):
        quads = [stage[b, pl.ds(8 + j, 16, stride=4)] for j in range(4)]
        blocks.append((quads[0] + quads[1]) + (quads[2] + quads[3]))
    pooled = jnp.concatenate(blocks, axis=1)
    crows, ccols = zc.shape[0], LANES // 4
    fine = lax.broadcasted_iota(jnp.int32, (2 * LANES, LANES), 0)
    cell = lax.broadcasted_iota(jnp.int32, (2 * LANES, LANES), 1)
    place = lax.shift_right_logical(fine, 2)
    hit = ((fine < LANES + 8) & (place == cell)) | ((fine >= 2 * LANES - 8) & (place - (2 * LANES // 4 - 2) == cell - (LANES - 2)))
    rc = jnp.dot(
        pooled,
        jnp.where(hit, 1.0, 0.0),
        precision=lax.Precision.HIGHEST,
        preferred_element_type=F32,
    ) * (INFILTRATION * TIME_STEP)

    has_north, has_south, has_east, has_west = flags
    rows = own.shape[1]
    odd = lax.axis_index("gy") % 2 == 1
    for k, middle in enumerate((coarse[...], east[rows : rows + crows], west[rows : rows + crows])):
        at = COARSE_AT + 2 * k
        cst[k] = jnp.zeros((16, LANES), F32)
        cst[k, 1:3] = rows_from(near, far, at, 2, odd, has_north)
        cst[k, 3 : 3 + crows] = middle
        cst[k, 3 + crows : 5 + crows] = rows_from(near, far, at, 2, ~odd, has_south)
    ids = lane_ids(16)
    e_here = (ids >= ccols) & (ids < jnp.where(has_east, ccols + 2, ccols))
    w_here = ids >= jnp.where(has_west, LANES - 2, LANES)
    pair = []
    for shift in (0, ccols):
        main = pltpu.roll(cst[0], LANES - shift, 1) if shift else cst[0]
        e = pltpu.roll(cst[1], (LANES + ccols - shift) % LANES, 1) if shift != ccols else cst[1]
        w = pltpu.roll(cst[2], (2 * LANES - ccols - shift) % LANES, 1)
        pair.append(jnp.where(ids < ccols, main, jnp.where(e_here, e, jnp.where(w_here, w, 0.0))))
    weight, pump = pair

    def beside(v):
        return (pltpu.roll(v, 1, 1) + pltpu.roll(v, LANES - 1, 1)) + (pltpu.roll(v, 1, 0) + pltpu.roll(v, 15, 0))

    drive = rc - pump
    z = weight * drive
    nz = beside(z)
    u = weight * nz
    nu = beside(u)
    mine = (ids < ccols)[3 : 3 + crows]
    cut = lambda v: v[3 : 3 + crows]
    z, nz, u, nu, drive = cut(z), cut(nz), cut(u), cut(nu), cut(drive)
    z = jnp.where(mine, z, 0.0)
    u = jnp.where(mine, u, 0.0)
    row = jnp.zeros((crows, LANES), F32)
    for k, (a, b) in enumerate(((drive, z), (z, nz), (u, nz), (u, nu))):
        part = a * b
        row = row + (pltpu.roll(part, k * ccols, 1) if k else part)
    row = jnp.sum(row, axis=0, keepdims=True)
    sums[...] = jnp.broadcast_to(row, sums.shape)
    zc[...] = z
    uc[...] = u


def state_kernel(counts, own, east, west, near, far, depth_out, tracers_out, stage, masks):
    flags = inside(counts)
    depth, rain, coef, codes, *species = gather_fields(
        (0, 1, 2, 3, 4, 5, 6), SLIM, own, east, west, near, far, flags, stage
    )
    move_masks(codes, coef, masks)

    def step(_, carry):
        now = carry[0]
        rate = speed(now, coef)
        flux = rate * now
        new = [now * KEEP - flux + rain + inflow(flux, masks)]
        for held in carry[1:]:
            flux = rate * held
            new.append(held * KEEP - flux + inflow(flux, masks))
        return tuple(new)

    final = lax.fori_loop(0, SUBSTEPS, step, (depth, *species))
    chunk = depth.shape[0]
    rows = own.shape[1]
    for k, field in enumerate(final):
        for i in range(chunk):
            stage[k, pl.ds(i, 8, stride=chunk)] = field[i, :, :LANES]
        if k == 0:
            depth_out[...] = stage[k, SLIM : SLIM + rows]
        else:
            tracers_out[k - 1] = stage[k, SLIM : SLIM + rows]


def head_kernel(sums, zc, uc, head):
    total = jnp.sum(sums[...], axis=0, keepdims=True)
    run = LANES // 4
    ids = lane_ids(1)
    n0, n1, n2, n3 = (
        jnp.sum(jnp.where((ids >= k * run) & (ids < (k + 1) * run), total, 0.0), axis=1, keepdims=True)
        for k in range(4)
    )
    pq = n0 - n1
    a0 = n0 / pq
    ratio = (n0 * n2 - n1 * n1) / (pq * pq)
    slope = (n1 - n2) / pq
    below = (n2 - n3) - slope * (n1 - n2)
    a1 = jnp.where(below > 0.0, n0 * ratio / jnp.where(below > 0.0, below, 1.0), 0.0) / a0
    wide = head.shape[1]
    head[...] = ((a0 - a1 * slope) * zc[...] + a1 * uc[...])[:, :wide]


def swaps(axis, offset, counts):
    pairs = []
    for col in range(counts[0]):
        for row in range(counts[1]):
            spot = [col, row]
            k = AXES.index(axis)
            other = ((spot[k] + offset) ^ 1) - offset
            if 0 <= other < counts[k]:
                spot[k] = other
            else:
                spot[1 - k] ^= 1
            pairs.append((col * counts[1] + row, spot[0] * counts[1] + spot[1]))
    return pairs


def exchange(near, far, axis, counts):
    near = lax.ppermute(near, AXES, swaps(axis, 0, counts))
    far = lax.ppermute(far, AXES, swaps(axis, 1, counts))
    return near, far


def shards(counts, *inputs):
    rows, cols = inputs[0].shape
    crows, ccols = inputs[6].shape
    shape = lambda *dims: jax.ShapeDtypeStruct(dims, F32)
    own, near, far, coarse = pl.pallas_call(
        pack_columns,
        out_shape=(shape(7, rows, cols), shape(rows + crows, LANES), shape(rows + crows, LANES), shape(crows, LANES)),
        in_specs=[pl.BlockSpec(memory_space=pltpu.MemorySpace.HBM)] * 9,
        out_specs=tuple(whole(4)),
        scratch_shapes=[pltpu.VMEM(a.shape, a.dtype) for a in inputs] + [pltpu.SemaphoreType.DMA((9,))],
        compiler_params=SMALL,
        name="pack_columns",
    )(*[pltpu.with_memory_space_constraint(a, pltpu.MemorySpace.HBM) for a in inputs])
    near, far = exchange(near, far, "gx", counts)
    near, far, east, west = pl.pallas_call(
        pack_rows,
        out_shape=(shape(STRIP, LANES), shape(STRIP, LANES), shape(rows + crows, LANES), shape(rows + crows, LANES)),
        in_specs=whole(4),
        out_specs=tuple(whole(4)),
        compiler_params=SMALL,
        name="pack_rows",
    )(own, near, far, coarse)
    near, far = exchange(near, far, "gy", counts)
    deep = rows + 2 * WIDE
    sums, zc, uc = pl.pallas_call(
        functools.partial(depth_kernel, counts),
        out_shape=(shape(counts[0] * counts[1], LANES), shape(crows, LANES), shape(crows, LANES)),
        in_specs=whole(6),
        out_specs=tuple(whole(3)),
        scratch_shapes=[
            pltpu.VMEM((9, deep, LANES), F32),
            pltpu.VMEM((8, deep // 8, 8, 2 * LANES), F32),
            pltpu.VMEM((3, 16, LANES), F32),
        ],
        compiler_params=ROOMY,
        name="depth_and_moments",
    )(own, east, west, near, far, coarse)
    low = rows + 2 * SLIM
    depth_out, tracers_out = pl.pallas_call(
        functools.partial(state_kernel, counts),
        out_shape=(shape(rows, cols), shape(3, rows, cols)),
        in_specs=whole(5),
        out_specs=tuple(whole(2)),
        scratch_shapes=[
            pltpu.VMEM((9, low, LANES), F32),
            pltpu.VMEM((8, low // 8, 8, 2 * LANES), F32),
        ],
        cost_estimate=pl.CostEstimate(flops=20_000_000, bytes_accessed=20_000_000, transcendentals=0),
        compiler_params=ROOMY,
        name="all_channels",
    )(own, east, west, near, far)
    sums = lax.all_to_all(sums, AXES, 0, 0, tiled=True)
    head = pl.pallas_call(
        head_kernel,
        out_shape=shape(crows, ccols),
        in_specs=whole(3),
        out_specs=pl.BlockSpec(memory_space=pltpu.VMEM),
        compiler_params=SMALL,
        name="combine_head",
    )(sums, zc, uc)
    return depth_out, tracers_out, head


def solution(mesh):
    counts = (mesh.shape["gx"], mesh.shape["gy"])
    tile = P("gy", "gx")
    deep = P(None, "gy", "gx")
    return jax.shard_map(
        functools.partial(shards, counts),
        mesh=mesh,
        in_specs=(tile, deep) + (tile,) * 7,
        out_specs=(tile, deep, tile),
        check_vma=False,
    )
```

```python
import functools

import jax
import jax.numpy as jnp
from jax import lax
from jax.experimental import pallas as pl
from jax.experimental.pallas import tpu as pltpu
from jax.sharding import PartitionSpec as P

SUBSTEPS = 12
TIME_STEP = 0.2
INFILTRATION = 0.05
MOVES = ((-1, -1), (-1, 0), (-1, 1), (0, -1), (0, 1), (1, -1), (1, 0), (1, 1))
AXES = ("gx", "gy")

WIDE = 20
SLIM = 12
LANES = 128
SLOTS = ((0, WIDE), (WIDE, WIDE), (2 * WIDE, WIDE), (3 * WIDE, WIDE)) + tuple(
    (4 * WIDE + k * SLIM, SLIM) for k in range(3)
)
EAST_AT = 4 * WIDE + 3 * SLIM
WEST_AT = EAST_AT + WIDE
COARSE_AT = WEST_AT + WIDE
STRIP = 168
F32 = jnp.float32
SMALL = pltpu.CompilerParams(vmem_limit_bytes=2 << 20)
ROOMY = pltpu.CompilerParams(vmem_limit_bytes=6 << 20)


def whole(count):
    return [pl.BlockSpec(memory_space=pltpu.VMEM)] * count


def lane_ids(rows):
    return lax.broadcasted_iota(jnp.int32, (rows, LANES), 1)


def pack_columns(*refs):
    sources, (own, near, far, coarse), buffers, done = refs[:9], refs[9:13], refs[13:22], refs[22]
    copies = [pltpu.make_async_copy(a, b, done.at[k]) for k, (a, b) in enumerate(zip(sources, buffers))]
    for copy in copies:
        copy.start()
    for copy in copies:
        copy.wait()
    depth, tracers, rain, rough, codes, land_mask, leak, pump, active = buffers
    land = land_mask[...].astype(F32)
    fields = [
        depth[...] * land,
        rain[...] * land * TIME_STEP,
        rough[...] * land * TIME_STEP,
        codes[...].astype(F32),
        tracers[0] * land,
        tracers[1] * land,
        tracers[2] * land,
    ]
    rows = land.shape[0]
    ids = lane_ids(rows)
    head = jnp.zeros((rows, LANES), F32)
    tail = jnp.zeros((rows, LANES), F32)
    for field, (at, width) in zip(fields, SLOTS):
        spot = (ids >= at) & (ids < at + width)
        head = jnp.where(spot, pltpu.roll(field, at, 1) if at else field, head)
        tail = jnp.where(spot, pltpu.roll(field, (at + width) % LANES, 1), tail)
    for k, field in enumerate(fields):
        own[k] = field
    act = active[...].astype(F32)
    weight = act / (act * (4.0 + leak[...]) + (1.0 - act))
    both = jnp.concatenate([weight, pump[...], jnp.zeros((act.shape[0], LANES - 2 * act.shape[1]), F32)], axis=1)
    coarse[...] = both
    odd = lax.axis_index("gx") % 2 == 1
    near[0:rows] = jnp.where(odd, head, tail)
    far[0:rows] = jnp.where(odd, tail, head)
    near[rows : rows + act.shape[0]] = both
    far[rows : rows + act.shape[0]] = both


def pack_rows(own, side_far, side_near, coarse, near, far, east, west):
    flip = lax.axis_index("gx") % 2 == 1
    east[...] = jnp.where(flip, side_far[...], side_near[...])
    west[...] = jnp.where(flip, side_near[...], side_far[...])
    rows = own.shape[1]
    crows = coarse.shape[0]
    odd = lax.axis_index("gy") % 2 == 1

    def put(at, top, bottom):
        near[at : at + top.shape[0]] = jnp.where(odd, top, bottom)
        far[at : at + top.shape[0]] = jnp.where(odd, bottom, top)

    for k, (at, width) in enumerate(SLOTS):
        put(at, own[k, 0:width], own[k, rows - width : rows])
    for at, side in ((EAST_AT, east), (WEST_AT, west)):
        put(at, side[0:WIDE], side[rows - WIDE : rows])
    for at, part in ((COARSE_AT, coarse), (COARSE_AT + 2, east.at[rows : rows + crows]), (COARSE_AT + 4, west.at[rows : rows + crows])):
        put(at, part[0:2], part[crows - 2 : crows])
    rest = jnp.zeros((STRIP - COARSE_AT - 6, LANES), F32)
    near[COARSE_AT + 6 : STRIP] = rest
    far[COARSE_AT + 6 : STRIP] = rest


def inside(counts):
    col = lax.axis_index("gx")
    row = lax.axis_index("gy")
    return row > 0, row < counts[1] - 1, col < counts[0] - 1, col > 0


def rows_from(near, far, start, count, use_near, present):
    got = jnp.where(use_near, near[start : start + count], far[start : start + count])
    return jnp.where(present, got, 0.0)


def gather_fields(kinds, halo, own, east, west, near, far, flags, stage):
    has_north, has_south, has_east, has_west = flags
    rows = own.shape[1]
    total = rows + 2 * halo
    chunk = total // 8
    odd = lax.axis_index("gy") % 2 == 1

    def lay(slot, at, width, middle):
        stage[slot, 0:halo] = rows_from(near, far, at + width - halo, halo, odd, has_north)
        stage[slot, halo : halo + rows] = middle
        stage[slot, halo + rows : total] = rows_from(near, far, at, halo, ~odd, has_south)

    def read(slot):
        return [stage[slot, pl.ds(i, 8, stride=chunk)] for i in range(chunk)]

    for k in kinds:
        at, width = SLOTS[k]
        lay(k, at, width, own[k])
    lay(7, EAST_AT, WIDE, east[0:rows])
    lay(8, WEST_AT, WIDE, west[0:rows])
    east_parts = read(7)
    west_parts = read(8)
    ids = lane_ids(8)
    fields = []
    for k in kinds:
        at, width = SLOTS[k]
        in_east = ids < jnp.where(has_east, width, 0)
        in_west = ids >= jnp.where(has_west, LANES - width, LANES)
        parts = []
        for main, e, w in zip(read(k), east_parts, west_parts):
            e = pltpu.roll(e, (LANES - at) % LANES, 1) if at else e
            w = pltpu.roll(w, (2 * LANES - width - at) % LANES, 1)
            side = jnp.where(in_east, e, jnp.where(in_west, w, 0.0))
            parts.append(jnp.concatenate([main, side], axis=1)[None])
        fields.append(jnp.concatenate(parts, axis=0))
    return fields


def from_left(field):
    return pltpu.roll(field, 1, 2)


def from_right(field):
    return pltpu.roll(field, field.shape[2] - 1, 2)


def from_above(field):
    return jnp.concatenate([pltpu.roll(field[-1], 1, 0)[None], field[:-1]], axis=0)


def from_below(field):
    return jnp.concatenate([field[1:], pltpu.roll(field[0], 7, 0)[None]], axis=0)


def move_masks(codes, coef, masks):
    land = coef > 0.0
    sides = {-1: from_right(codes), 0: codes, 1: from_left(codes)}
    for k, (drow, dcol) in enumerate(MOVES):
        seen = sides[dcol]
        if drow == 1:
            seen = from_above(seen)
        elif drow == -1:
            seen = from_below(seen)
        masks[k] = jnp.where(land & (seen == float(k)), 1.0, 0.0)


def inflow(flux, masks):
    sides = {-1: from_right(flux), 0: flux, 1: from_left(flux)}
    total = None
    for dcol in (0, 1, -1):
        side = sides[dcol]
        for drow, seen in ((0, side), (1, from_above(side)), (-1, from_below(side))):
            if (drow, dcol) == (0, 0):
                continue
            term = masks[MOVES.index((drow, dcol))] * seen
            total = term if total is None else total + term
    return total


def speed(depth, coef):
    return coef * jnp.exp(jnp.log(jnp.abs(depth)) * (2.0 / 3.0))


KEEP = 1.0 - TIME_STEP * INFILTRATION


def depth_kernel(counts, own, east, west, far, near, coarse, sums, zc, uc, stage, masks, cst):
    flags = inside(counts)
    depth, rain, coef, codes = gather_fields((0, 1, 2, 3), WIDE, own, east, west, near, far, flags, stage)
    move_masks(codes, coef, masks)

    crows, ccols = zc.shape[0], LANES // 4
    fine = lax.broadcasted_iota(jnp.int32, (2 * LANES, LANES), 0)
    cell = lax.broadcasted_iota(jnp.int32, (2 * LANES, LANES), 1)
    place = lax.shift_right_logical(fine, 2)
    hit = ((fine < LANES + 8) & (place == cell)) | ((fine >= 2 * LANES - 8) & (place - (2 * LANES // 4 - 2) == cell - (LANES - 2)))
    pick = jnp.where(hit, 1.0, 0.0)
    has_north, has_south, has_east, has_west = flags
    rows = own.shape[1]
    odd = lax.axis_index("gy") % 2 == 1
    for k, middle in enumerate((coarse[...], east[rows : rows + crows], west[rows : rows + crows])):
        at = COARSE_AT + 2 * k
        cst[k] = jnp.zeros((16, LANES), F32)
        cst[k, 1:3] = rows_from(near, far, at, 2, odd, has_north)
        cst[k, 3 : 3 + crows] = middle
        cst[k, 3 + crows : 5 + crows] = rows_from(near, far, at, 2, ~odd, has_south)
    ids = lane_ids(16)
    e_here = (ids >= ccols) & (ids < jnp.where(has_east, ccols + 2, ccols))
    w_here = ids >= jnp.where(has_west, LANES - 2, LANES)
    pair = []
    for shift in (0, ccols):
        main = pltpu.roll(cst[0], LANES - shift, 1) if shift else cst[0]
        e = pltpu.roll(cst[1], (LANES + ccols - shift) % LANES, 1) if shift != ccols else cst[1]
        w = pltpu.roll(cst[2], (2 * LANES - ccols - shift) % LANES, 1)
        pair.append(jnp.where(ids < ccols, main, jnp.where(e_here, e, jnp.where(w_here, w, 0.0))))
    weight, pump = pair


    def step(_, carry):
        now, total = carry
        flux = speed(now, coef) * now
        return now * KEEP - flux + rain + inflow(flux, masks), total + now

    now, total = lax.fori_loop(0, SUBSTEPS - 1, step, (depth, jnp.zeros_like(depth)), unroll=True)
    total = total + now
    chunk = total.shape[0]
    for i in range(chunk):
        stage[0, pl.ds(i, 8, stride=chunk)] = total[i, :, :LANES]
        stage[1, pl.ds(i, 8, stride=chunk)] = total[i, :, LANES:]
    blocks = []
    for b in range(2):
        quads = [stage[b, pl.ds(8 + j, 16, stride=4)] for j in range(4)]
        blocks.append((quads[0] + quads[1]) + (quads[2] + quads[3]))
    pooled = jnp.concatenate(blocks, axis=1)
    rc = jnp.dot(
        pooled,
        pick,
        precision=lax.Precision.HIGHEST,
        preferred_element_type=F32,
    ) * (INFILTRATION * TIME_STEP)

    def beside(v):
        return (pltpu.roll(v, 1, 1) + pltpu.roll(v, LANES - 1, 1)) + (pltpu.roll(v, 1, 0) + pltpu.roll(v, 15, 0))

    drive = rc - pump
    z = weight * drive
    nz = beside(z)
    u = weight * nz
    nu = beside(u)
    mine = (ids < ccols)[3 : 3 + crows]
    cut = lambda v: v[3 : 3 + crows]
    z, nz, u, nu, drive = cut(z), cut(nz), cut(u), cut(nu), cut(drive)
    z = jnp.where(mine, z, 0.0)
    u = jnp.where(mine, u, 0.0)
    row = jnp.zeros((crows, LANES), F32)
    for k, (a, b) in enumerate(((drive, z), (z, nz), (u, nz), (u, nu))):
        part = a * b
        row = row + (pltpu.roll(part, k * ccols, 1) if k else part)
    row = jnp.sum(row, axis=0, keepdims=True)
    sums[...] = jnp.broadcast_to(row, sums.shape)
    zc[...] = z
    uc[...] = u


def state_kernel(counts, own, east, west, far, near, depth_out, tracers_out, stage, masks):
    flags = inside(counts)
    depth, rain, coef, codes, *species = gather_fields(
        (0, 1, 2, 3, 4, 5, 6), SLIM, own, east, west, near, far, flags, stage
    )
    move_masks(codes, coef, masks)

    def step(_, carry):
        now = carry[0]
        rate = speed(now, coef)
        flux = rate * now
        new = [now * KEEP - flux + rain + inflow(flux, masks)]
        for held in carry[1:]:
            flux = rate * held
            new.append(held * KEEP - flux + inflow(flux, masks))
        return tuple(new)

    final = lax.fori_loop(0, SUBSTEPS, step, (depth, *species), unroll=4)
    chunk = depth.shape[0]
    rows = own.shape[1]
    for k, field in enumerate(final):
        for i in range(chunk):
            stage[k, pl.ds(i, 8, stride=chunk)] = field[i, :, :LANES]
        if k == 0:
            depth_out[...] = stage[k, SLIM : SLIM + rows]
        else:
            tracers_out[k - 1] = stage[k, SLIM : SLIM + rows]


def head_kernel(sums, zc, uc, head):
    total = jnp.sum(sums[...], axis=0, keepdims=True)
    run = LANES // 4
    ids = lane_ids(1)
    n0, n1, n2, n3 = (
        jnp.sum(jnp.where((ids >= k * run) & (ids < (k + 1) * run), total, 0.0), axis=1, keepdims=True)
        for k in range(4)
    )
    pq = n0 - n1
    a0 = n0 / pq
    ratio = (n0 * n2 - n1 * n1) / (pq * pq)
    slope = (n1 - n2) / pq
    below = (n2 - n3) - slope * (n1 - n2)
    a1 = jnp.where(below > 0.0, n0 * ratio / jnp.where(below > 0.0, below, 1.0), 0.0) / a0
    wide = head.shape[1]
    head[...] = ((a0 - a1 * slope) * zc[...] + a1 * uc[...])[:, :wide]


def swaps(axis, offset, counts):
    pairs = []
    for col in range(counts[0]):
        for row in range(counts[1]):
            spot = [col, row]
            k = AXES.index(axis)
            other = ((spot[k] + offset) ^ 1) - offset
            if 0 <= other < counts[k]:
                spot[k] = other
            else:
                spot[1 - k] ^= 1
            pairs.append((col * counts[1] + row, spot[0] * counts[1] + spot[1]))
    return pairs


def exchange(near, far, axis, counts):
    near = lax.ppermute(near, AXES, swaps(axis, 0, counts))
    far = lax.ppermute(far, AXES, swaps(axis, 1, counts))
    return near, far


def shards(counts, *inputs):
    rows, cols = inputs[0].shape
    crows, ccols = inputs[6].shape
    shape = lambda *dims: jax.ShapeDtypeStruct(dims, F32)
    own, near, far, coarse = pl.pallas_call(
        pack_columns,
        out_shape=(shape(7, rows, cols), shape(rows + crows, LANES), shape(rows + crows, LANES), shape(crows, LANES)),
        in_specs=[pl.BlockSpec(memory_space=pltpu.MemorySpace.HBM)] * 9,
        out_specs=tuple(whole(4)),
        scratch_shapes=[pltpu.VMEM(a.shape, a.dtype) for a in inputs] + [pltpu.SemaphoreType.DMA((9,))],
        compiler_params=SMALL,
        name="pack_columns",
    )(*[pltpu.with_memory_space_constraint(a, pltpu.MemorySpace.HBM) for a in inputs])
    near, far = exchange(near, far, "gx", counts)
    near, far, east, west = pl.pallas_call(
        pack_rows,
        out_shape=(shape(STRIP, LANES), shape(STRIP, LANES), shape(rows + crows, LANES), shape(rows + crows, LANES)),
        in_specs=whole(4),
        out_specs=tuple(whole(4)),
        compiler_params=SMALL,
        name="pack_rows",
    )(own, far, near, coarse)
    near, far = exchange(near, far, "gy", counts)
    deep = rows + 2 * WIDE
    sums, zc, uc = pl.pallas_call(
        functools.partial(depth_kernel, counts),
        out_shape=(shape(counts[0] * counts[1], LANES), shape(crows, LANES), shape(crows, LANES)),
        in_specs=whole(6),
        out_specs=tuple(whole(3)),
        scratch_shapes=[
            pltpu.VMEM((9, deep, LANES), F32),
            pltpu.VMEM((8, deep // 8, 8, 2 * LANES), F32),
            pltpu.VMEM((3, 16, LANES), F32),
        ],
        compiler_params=ROOMY,
        name="depth_and_moments",
    )(own, east, west, far, near, coarse)
    low = rows + 2 * SLIM
    depth_out, tracers_out = pl.pallas_call(
        functools.partial(state_kernel, counts),
        out_shape=(shape(rows, cols), shape(3, rows, cols)),
        in_specs=whole(5),
        out_specs=tuple(whole(2)),
        scratch_shapes=[
            pltpu.VMEM((9, low, LANES), F32),
            pltpu.VMEM((8, low // 8, 8, 2 * LANES), F32),
        ],
        cost_estimate=pl.CostEstimate(flops=20_000_000, bytes_accessed=20_000_000, transcendentals=0),
        compiler_params=ROOMY,
        name="all_channels",
    )(own, east, west, far, near)
    sums = lax.all_to_all(sums, AXES, 0, 0, tiled=True)
    head = pl.pallas_call(
        head_kernel,
        out_shape=shape(crows, ccols),
        in_specs=whole(3),
        out_specs=pl.BlockSpec(memory_space=pltpu.VMEM),
        compiler_params=SMALL,
        name="combine_head",
    )(sums, zc, uc)
    return depth_out, tracers_out, head


def solution(mesh):
    counts = (mesh.shape["gx"], mesh.shape["gy"])
    tile = P("gy", "gx")
    deep = P(None, "gy", "gx")
    return jax.shard_map(
        functools.partial(shards, counts),
        mesh=mesh,
        in_specs=(tile, deep) + (tile,) * 7,
        out_specs=(tile, deep, tile),
        check_vma=False,
    )
```

```python
import functools

import jax
import jax.numpy as jnp
from jax import lax
from jax.experimental import pallas as pl
from jax.experimental.pallas import tpu as pltpu
from jax.sharding import PartitionSpec as P

SUBSTEPS = 12
TIME_STEP = 0.2
INFILTRATION = 0.05
MOVES = ((-1, -1), (-1, 0), (-1, 1), (0, -1), (0, 1), (1, -1), (1, 0), (1, 1))
AXES = ("gx", "gy")

WIDE = 20
SLIM = 12
LANES = 128
SLOTS = ((0, WIDE), (WIDE, WIDE), (2 * WIDE, WIDE), (3 * WIDE, WIDE)) + tuple(
    (4 * WIDE + k * SLIM, SLIM) for k in range(3)
)
EAST_AT = 4 * WIDE
WEST_AT = EAST_AT + WIDE
COARSE_AT = WEST_AT + WIDE
EARLY = 128
ROWS_AT = (0, WIDE, 2 * WIDE, 3 * WIDE) + tuple(EARLY + k * SLIM for k in range(3))
STRIP = 168
F32 = jnp.float32
SMALL = pltpu.CompilerParams(vmem_limit_bytes=2 << 20)
ROOMY = pltpu.CompilerParams(vmem_limit_bytes=6 << 20)


def whole(count):
    return [pl.BlockSpec(memory_space=pltpu.VMEM)] * count


def lane_ids(rows):
    return lax.broadcasted_iota(jnp.int32, (rows, LANES), 1)


def pack_columns(*refs):
    sources, (own, near, far, coarse), buffers, done = refs[:9], refs[9:13], refs[13:22], refs[22]
    copies = [pltpu.make_async_copy(a, b, done.at[k]) for k, (a, b) in enumerate(zip(sources, buffers))]
    for copy in copies:
        copy.start()
    for copy in copies:
        copy.wait()
    depth, tracers, rain, rough, codes, land_mask, leak, pump, active = buffers
    land = land_mask[...].astype(F32)
    fields = [
        depth[...] * land,
        rain[...] * land * TIME_STEP,
        rough[...] * land * TIME_STEP,
        codes[...].astype(F32),
        tracers[0] * land,
        tracers[1] * land,
        tracers[2] * land,
    ]
    rows = land.shape[0]
    ids = lane_ids(rows)
    head = jnp.zeros((rows, LANES), F32)
    tail = jnp.zeros((rows, LANES), F32)
    for field, (at, width) in zip(fields, SLOTS):
        spot = (ids >= at) & (ids < at + width)
        head = jnp.where(spot, pltpu.roll(field, at, 1) if at else field, head)
        tail = jnp.where(spot, pltpu.roll(field, (at + width) % LANES, 1), tail)
    for k, field in enumerate(fields):
        own[k] = field
    act = active[...].astype(F32)
    weight = act / (act * (4.0 + leak[...]) + (1.0 - act))
    both = jnp.concatenate([weight, pump[...], jnp.zeros((act.shape[0], LANES - 2 * act.shape[1]), F32)], axis=1)
    coarse[...] = both
    odd = lax.axis_index("gx") % 2 == 1
    near[0:rows] = jnp.where(odd, head, tail)
    far[0:rows] = jnp.where(odd, tail, head)
    near[rows : rows + act.shape[0]] = both
    far[rows : rows + act.shape[0]] = both


def pack_rows(own, side_far, side_near, coarse, near, far, near_late, far_late, east, west):
    flip = lax.axis_index("gx") % 2 == 1
    east[...] = jnp.where(flip, side_far[...], side_near[...])
    west[...] = jnp.where(flip, side_near[...], side_far[...])
    rows = own.shape[1]
    crows = coarse.shape[0]
    odd = lax.axis_index("gy") % 2 == 1

    def put(at, top, bottom):
        count = top.shape[0]
        early = at < EARLY
        at = at if early else at - EARLY
        (near if early else near_late)[at : at + count] = jnp.where(odd, top, bottom)
        (far if early else far_late)[at : at + count] = jnp.where(odd, bottom, top)

    for k, at in enumerate(ROWS_AT):
        width = SLOTS[k][1]
        put(at, own[k, 0:width], own[k, rows - width : rows])
    for at, side in ((EAST_AT, east), (WEST_AT, west)):
        put(at, side[0:WIDE], side[rows - WIDE : rows])
    for k, part in enumerate((coarse, east.at[rows : rows + crows], west.at[rows : rows + crows])):
        put(COARSE_AT + 2 * k, part[0:2], part[crows - 2 : crows])
    for start, stop in ((COARSE_AT + 6, EARLY), (ROWS_AT[-1] + SLIM, STRIP)):
        rest = jnp.zeros((stop - start, LANES), F32)
        put(start, rest, rest)


def inside(counts):
    col = lax.axis_index("gx")
    row = lax.axis_index("gy")
    return row > 0, row < counts[1] - 1, col < counts[0] - 1, col > 0


def rows_from(near, far, late, start, count, use_near, present):
    if start >= EARLY:
        (near, far), start = late, start - EARLY
    got = jnp.where(use_near, near[start : start + count], far[start : start + count])
    return jnp.where(present, got, 0.0)


def gather_fields(kinds, halo, own, east, west, near, far, late, flags, stage):
    has_north, has_south, has_east, has_west = flags
    rows = own.shape[1]
    total = rows + 2 * halo
    chunk = total // 8
    odd = lax.axis_index("gy") % 2 == 1

    def lay(slot, at, width, middle):
        stage[slot, 0:halo] = rows_from(near, far, late, at + width - halo, halo, odd, has_north)
        stage[slot, halo : halo + rows] = middle
        stage[slot, halo + rows : total] = rows_from(near, far, late, at, halo, ~odd, has_south)

    def read(slot):
        return [stage[slot, pl.ds(i, 8, stride=chunk)] for i in range(chunk)]

    for k in kinds:
        lay(k, ROWS_AT[k], SLOTS[k][1], own[k])
    lay(7, EAST_AT, WIDE, east[0:rows])
    lay(8, WEST_AT, WIDE, west[0:rows])
    east_parts = read(7)
    west_parts = read(8)
    ids = lane_ids(8)
    fields = []
    for k in kinds:
        at, width = SLOTS[k]
        in_east = ids < jnp.where(has_east, width, 0)
        in_west = ids >= jnp.where(has_west, LANES - width, LANES)
        parts = []
        for main, e, w in zip(read(k), east_parts, west_parts):
            e = pltpu.roll(e, (LANES - at) % LANES, 1) if at else e
            w = pltpu.roll(w, (2 * LANES - width - at) % LANES, 1)
            side = jnp.where(in_east, e, jnp.where(in_west, w, 0.0))
            parts.append(jnp.concatenate([main, side], axis=1)[None])
        fields.append(jnp.concatenate(parts, axis=0))
    return fields


def from_left(field):
    return pltpu.roll(field, 1, 2)


def from_right(field):
    return pltpu.roll(field, field.shape[2] - 1, 2)


def from_above(field):
    return jnp.concatenate([pltpu.roll(field[-1], 1, 0)[None], field[:-1]], axis=0)


def from_below(field):
    return jnp.concatenate([field[1:], pltpu.roll(field[0], 7, 0)[None]], axis=0)


def move_masks(codes, coef, masks):
    land = coef > 0.0
    sides = {-1: from_right(codes), 0: codes, 1: from_left(codes)}
    for k, (drow, dcol) in enumerate(MOVES):
        seen = sides[dcol]
        if drow == 1:
            seen = from_above(seen)
        elif drow == -1:
            seen = from_below(seen)
        masks[k] = jnp.where(land & (seen == float(k)), 1.0, 0.0)


def inflow(flux, masks):
    sides = {-1: from_right(flux), 0: flux, 1: from_left(flux)}
    total = None
    for dcol in (0, 1, -1):
        side = sides[dcol]
        for drow, seen in ((0, side), (1, from_above(side)), (-1, from_below(side))):
            if (drow, dcol) == (0, 0):
                continue
            term = masks[MOVES.index((drow, dcol))] * seen
            total = term if total is None else total + term
    return total


def speed(depth, coef):
    return coef * jnp.exp(jnp.log(jnp.abs(depth)) * (2.0 / 3.0))


KEEP = 1.0 - TIME_STEP * INFILTRATION


def depth_kernel(counts, own, east, west, near, far, coarse, sums, zc, uc, stage, masks, cst):
    flags = inside(counts)
    depth, rain, coef, codes = gather_fields((0, 1, 2, 3), WIDE, own, east, west, near, far, None, flags, stage)
    move_masks(codes, coef, masks)

    crows, ccols = zc.shape[0], LANES // 4
    fine = lax.broadcasted_iota(jnp.int32, (2 * LANES, LANES), 0)
    cell = lax.broadcasted_iota(jnp.int32, (2 * LANES, LANES), 1)
    place = lax.shift_right_logical(fine, 2)
    hit = ((fine < LANES + 8) & (place == cell)) | ((fine >= 2 * LANES - 8) & (place - (2 * LANES // 4 - 2) == cell - (LANES - 2)))
    pick = jnp.where(hit, 1.0, 0.0)
    has_north, has_south, has_east, has_west = flags
    rows = own.shape[1]
    odd = lax.axis_index("gy") % 2 == 1
    for k, middle in enumerate((coarse[...], east[rows : rows + crows], west[rows : rows + crows])):
        at = COARSE_AT + 2 * k
        cst[k] = jnp.zeros((16, LANES), F32)
        cst[k, 1:3] = rows_from(near, far, None, at, 2, odd, has_north)
        cst[k, 3 : 3 + crows] = middle
        cst[k, 3 + crows : 5 + crows] = rows_from(near, far, None, at, 2, ~odd, has_south)
    ids = lane_ids(16)
    e_here = (ids >= ccols) & (ids < jnp.where(has_east, ccols + 2, ccols))
    w_here = ids >= jnp.where(has_west, LANES - 2, LANES)
    pair = []
    for shift in (0, ccols):
        main = pltpu.roll(cst[0], LANES - shift, 1) if shift else cst[0]
        e = pltpu.roll(cst[1], (LANES + ccols - shift) % LANES, 1) if shift != ccols else cst[1]
        w = pltpu.roll(cst[2], (2 * LANES - ccols - shift) % LANES, 1)
        pair.append(jnp.where(ids < ccols, main, jnp.where(e_here, e, jnp.where(w_here, w, 0.0))))
    weight, pump = pair


    def step(_, carry):
        now, total = carry
        flux = speed(now, coef) * now
        return now * KEEP - flux + rain + inflow(flux, masks), total + now

    now, total = lax.fori_loop(0, SUBSTEPS - 1, step, (depth, jnp.zeros_like(depth)), unroll=True)
    total = total + now
    chunk = total.shape[0]
    for i in range(chunk):
        stage[0, pl.ds(i, 8, stride=chunk)] = total[i, :, :LANES]
        stage[1, pl.ds(i, 8, stride=chunk)] = total[i, :, LANES:]
    blocks = []
    for b in range(2):
        quads = [stage[b, pl.ds(8 + j, 16, stride=4)] for j in range(4)]
        blocks.append((quads[0] + quads[1]) + (quads[2] + quads[3]))
    pooled = jnp.concatenate(blocks, axis=1)
    rc = jnp.dot(
        pooled,
        pick,
        precision=lax.Precision.HIGHEST,
        preferred_element_type=F32,
    ) * (INFILTRATION * TIME_STEP)

    def beside(v):
        return (pltpu.roll(v, 1, 1) + pltpu.roll(v, LANES - 1, 1)) + (pltpu.roll(v, 1, 0) + pltpu.roll(v, 15, 0))

    drive = rc - pump
    z = weight * drive
    nz = beside(z)
    u = weight * nz
    nu = beside(u)
    mine = (ids < ccols)[3 : 3 + crows]
    cut = lambda v: v[3 : 3 + crows]
    z, nz, u, nu, drive = cut(z), cut(nz), cut(u), cut(nu), cut(drive)
    z = jnp.where(mine, z, 0.0)
    u = jnp.where(mine, u, 0.0)
    row = jnp.zeros((crows, LANES), F32)
    for k, (a, b) in enumerate(((drive, z), (z, nz), (u, nz), (u, nu))):
        part = a * b
        row = row + (pltpu.roll(part, k * ccols, 1) if k else part)
    row = jnp.sum(row, axis=0, keepdims=True)
    sums[...] = jnp.broadcast_to(row, sums.shape)
    zc[...] = z
    uc[...] = u


def state_kernel(counts, own, east, west, far, near, far_late, near_late, depth_out, tracers_out, stage, masks):
    flags = inside(counts)
    depth, rain, coef, codes, *species = gather_fields(
        (0, 1, 2, 3, 4, 5, 6), SLIM, own, east, west, near, far, (near_late, far_late), flags, stage
    )
    move_masks(codes, coef, masks)

    def step(_, carry):
        now = carry[0]
        rate = speed(now, coef)
        flux = rate * now
        new = [now * KEEP - flux + rain + inflow(flux, masks)]
        for held in carry[1:]:
            flux = rate * held
            new.append(held * KEEP - flux + inflow(flux, masks))
        return tuple(new)

    final = lax.fori_loop(0, SUBSTEPS, step, (depth, *species), unroll=4)
    chunk = depth.shape[0]
    rows = own.shape[1]
    for k, field in enumerate(final):
        for i in range(chunk):
            stage[k, pl.ds(i, 8, stride=chunk)] = field[i, :, :LANES]
        if k == 0:
            depth_out[...] = stage[k, SLIM : SLIM + rows]
        else:
            tracers_out[k - 1] = stage[k, SLIM : SLIM + rows]


def head_kernel(sums, zc, uc, head):
    total = jnp.sum(sums[...], axis=0, keepdims=True)
    run = LANES // 4
    ids = lane_ids(1)
    n0, n1, n2, n3 = (
        jnp.sum(jnp.where((ids >= k * run) & (ids < (k + 1) * run), total, 0.0), axis=1, keepdims=True)
        for k in range(4)
    )
    pq = n0 - n1
    a0 = n0 / pq
    ratio = (n0 * n2 - n1 * n1) / (pq * pq)
    slope = (n1 - n2) / pq
    below = (n2 - n3) - slope * (n1 - n2)
    a1 = jnp.where(below > 0.0, n0 * ratio / jnp.where(below > 0.0, below, 1.0), 0.0) / a0
    wide = head.shape[1]
    head[...] = ((a0 - a1 * slope) * zc[...] + a1 * uc[...])[:, :wide]


def swaps(axis, offset, counts):
    pairs = []
    for col in range(counts[0]):
        for row in range(counts[1]):
            spot = [col, row]
            k = AXES.index(axis)
            other = ((spot[k] + offset) ^ 1) - offset
            if 0 <= other < counts[k]:
                spot[k] = other
            else:
                spot[1 - k] ^= 1
            pairs.append((col * counts[1] + row, spot[0] * counts[1] + spot[1]))
    return pairs


def exchange(near, far, axis, counts):
    near = lax.ppermute(near, AXES, swaps(axis, 0, counts))
    far = lax.ppermute(far, AXES, swaps(axis, 1, counts))
    return near, far


def shards(counts, *inputs):
    rows, cols = inputs[0].shape
    crows, ccols = inputs[6].shape
    shape = lambda *dims: jax.ShapeDtypeStruct(dims, F32)
    own, near, far, coarse = pl.pallas_call(
        pack_columns,
        out_shape=(shape(7, rows, cols), shape(rows + crows, LANES), shape(rows + crows, LANES), shape(crows, LANES)),
        in_specs=[pl.BlockSpec(memory_space=pltpu.MemorySpace.HBM)] * 9,
        out_specs=tuple(whole(4)),
        scratch_shapes=[pltpu.VMEM(a.shape, a.dtype) for a in inputs] + [pltpu.SemaphoreType.DMA((9,))],
        compiler_params=SMALL,
        name="pack_columns",
    )(*[pltpu.with_memory_space_constraint(a, pltpu.MemorySpace.HBM) for a in inputs])
    near, far = exchange(near, far, "gx", counts)
    near, far, near_late, far_late, east, west = pl.pallas_call(
        pack_rows,
        out_shape=(
            shape(EARLY, LANES),
            shape(EARLY, LANES),
            shape(STRIP - EARLY, LANES),
            shape(STRIP - EARLY, LANES),
            shape(rows + crows, LANES),
            shape(rows + crows, LANES),
        ),
        in_specs=whole(4),
        out_specs=tuple(whole(6)),
        compiler_params=SMALL,
        name="pack_rows",
    )(own, far, near, coarse)
    near, far = exchange(near, far, "gy", counts)
    near_late, far_late = exchange(near_late, far_late, "gy", counts)
    deep = rows + 2 * WIDE
    sums, zc, uc = pl.pallas_call(
        functools.partial(depth_kernel, counts),
        out_shape=(shape(counts[0] * counts[1], LANES), shape(crows, LANES), shape(crows, LANES)),
        in_specs=whole(6),
        out_specs=tuple(whole(3)),
        scratch_shapes=[
            pltpu.VMEM((9, deep, LANES), F32),
            pltpu.VMEM((8, deep // 8, 8, 2 * LANES), F32),
            pltpu.VMEM((3, 16, LANES), F32),
        ],
        compiler_params=ROOMY,
        cost_estimate=pl.CostEstimate(flops=20000000, bytes_accessed=20000000, transcendentals=0),
        name="depth_and_moments",
    )(own, east, west, near, far, coarse)
    sums, near_late, far_late = lax.optimization_barrier((sums, near_late, far_late))
    low = rows + 2 * SLIM
    depth_out, tracers_out = pl.pallas_call(
        functools.partial(state_kernel, counts),
        out_shape=(shape(rows, cols), shape(3, rows, cols)),
        in_specs=whole(7),
        out_specs=tuple(whole(2)),
        scratch_shapes=[
            pltpu.VMEM((9, low, LANES), F32),
            pltpu.VMEM((8, low // 8, 8, 2 * LANES), F32),
        ],
        cost_estimate=pl.CostEstimate(flops=20_000_000, bytes_accessed=20_000_000, transcendentals=0),
        compiler_params=ROOMY,
        name="all_channels",
    )(own, east, west, far, near, far_late, near_late)
    sums = lax.all_to_all(sums, AXES, 0, 0, tiled=True)
    head = pl.pallas_call(
        head_kernel,
        out_shape=shape(crows, ccols),
        in_specs=whole(3),
        out_specs=pl.BlockSpec(memory_space=pltpu.VMEM),
        compiler_params=SMALL,
        name="combine_head",
    )(sums, zc, uc)
    return depth_out, tracers_out, head


def solution(mesh):
    counts = (mesh.shape["gx"], mesh.shape["gy"])
    tile = P("gy", "gx")
    deep = P(None, "gy", "gx")
    return jax.shard_map(
        functools.partial(shards, counts),
        mesh=mesh,
        in_specs=(tile, deep) + (tile,) * 7,
        out_specs=(tile, deep, tile),
        check_vma=False,
    )
```

```python
import functools

import jax
import jax.numpy as jnp
from jax import lax
from jax.experimental import pallas as pl
from jax.experimental.pallas import tpu as pltpu
from jax.sharding import PartitionSpec as P

SUBSTEPS = 12
TIME_STEP = 0.2
INFILTRATION = 0.05
MOVES = ((-1, -1), (-1, 0), (-1, 1), (0, -1), (0, 1), (1, -1), (1, 0), (1, 1))
AXES = ("gx", "gy")

WIDE = 20
SLIM = 12
LANES = 128
SLOTS = ((0, WIDE), (WIDE, WIDE), (2 * WIDE, WIDE), (3 * WIDE, WIDE)) + tuple(
    (4 * WIDE + k * SLIM, SLIM) for k in range(3)
)
EAST_AT = 4 * WIDE
WEST_AT = EAST_AT + WIDE
COARSE_AT = WEST_AT + WIDE
EARLY = 128
ROWS_AT = (0, WIDE, 2 * WIDE, 3 * WIDE) + tuple(EARLY + k * SLIM for k in range(3))
STRIP = 168
F32 = jnp.float32
SMALL = pltpu.CompilerParams(vmem_limit_bytes=2 << 20)
ROOMY = pltpu.CompilerParams(vmem_limit_bytes=6 << 20)


def whole(count):
    return [pl.BlockSpec(memory_space=pltpu.VMEM)] * count


def run(ids, start, width, present):
    start = start % LANES
    return (ids >= start) & (ids < (start + width if present is True else jnp.where(present, start + width, start)))


def lane_ids(rows):
    return lax.broadcasted_iota(jnp.int32, (rows, LANES), 1)


def pack_columns(*refs):
    sources, (own, near, far, coarse), buffers, done = refs[:9], refs[9:13], refs[13:22], refs[22]
    copies = [pltpu.make_async_copy(a, b, done.at[k]) for k, (a, b) in enumerate(zip(sources, buffers))]
    for copy in copies:
        copy.start()
    for copy in copies:
        copy.wait()
    depth, tracers, rain, rough, codes, land_mask, leak, pump, active = buffers
    land = land_mask[...].astype(F32)
    fields = [
        depth[...] * land,
        rain[...] * land * TIME_STEP,
        rough[...] * land * TIME_STEP,
        codes[...].astype(F32),
        tracers[0] * land,
        tracers[1] * land,
        tracers[2] * land,
    ]
    rows = land.shape[0]
    ids = lane_ids(rows)
    head = jnp.zeros((rows, LANES), F32)
    tail = jnp.zeros((rows, LANES), F32)
    for field, (at, width) in zip(fields, SLOTS):
        moved = pltpu.roll(field, at, 1) if at else field
        head = jnp.where(run(ids, at, width, True), moved, head)
        tail = jnp.where(run(ids, at - width, width, True), moved, tail)
    for k, field in enumerate(fields):
        own[k] = field
    act = active[...].astype(F32)
    weight = act / (act * (4.0 + leak[...]) + (1.0 - act))
    both = jnp.concatenate([weight, pump[...], jnp.zeros((act.shape[0], LANES - 2 * act.shape[1]), F32)], axis=1)
    coarse[...] = both
    odd = lax.axis_index("gx") % 2 == 1
    near[0:rows] = jnp.where(odd, head, tail)
    far[0:rows] = jnp.where(odd, tail, head)
    near[rows : rows + act.shape[0]] = both
    far[rows : rows + act.shape[0]] = both


def pack_rows(own, side_far, side_near, coarse, near, far, near_late, far_late, east, west):
    flip = lax.axis_index("gx") % 2 == 1
    east[...] = jnp.where(flip, side_far[...], side_near[...])
    west[...] = jnp.where(flip, side_near[...], side_far[...])
    rows = own.shape[1]
    crows = coarse.shape[0]
    odd = lax.axis_index("gy") % 2 == 1

    def put(at, top, bottom):
        count = top.shape[0]
        early = at < EARLY
        at = at if early else at - EARLY
        (near if early else near_late)[at : at + count] = jnp.where(odd, top, bottom)
        (far if early else far_late)[at : at + count] = jnp.where(odd, bottom, top)

    for k, at in enumerate(ROWS_AT):
        width = SLOTS[k][1]
        put(at, own[k, 0:width], own[k, rows - width : rows])
    for at, side in ((EAST_AT, east), (WEST_AT, west)):
        put(at, side[0:WIDE], side[rows - WIDE : rows])
    for k, part in enumerate((coarse, east.at[rows : rows + crows], west.at[rows : rows + crows])):
        put(COARSE_AT + 2 * k, part[0:2], part[crows - 2 : crows])
    for start, stop in ((COARSE_AT + 6, EARLY), (ROWS_AT[-1] + SLIM, STRIP)):
        rest = jnp.zeros((stop - start, LANES), F32)
        put(start, rest, rest)


def inside(counts):
    col = lax.axis_index("gx")
    row = lax.axis_index("gy")
    return row > 0, row < counts[1] - 1, col < counts[0] - 1, col > 0


def rows_from(near, far, late, start, count, use_near, present):
    if start >= EARLY:
        (near, far), start = late, start - EARLY
    got = jnp.where(use_near, near[start : start + count], far[start : start + count])
    return jnp.where(present, got, 0.0)


def gather_fields(kinds, halo, own, east, west, near, far, late, flags, stage):
    has_north, has_south, has_east, has_west = flags
    rows = own.shape[1]
    total = rows + 2 * halo
    chunk = total // 8
    odd = lax.axis_index("gy") % 2 == 1

    def lay(slot, at, width, middle):
        stage[slot, 0:halo] = rows_from(near, far, late, at + width - halo, halo, odd, has_north)
        stage[slot, halo : halo + rows] = middle
        stage[slot, halo + rows : total] = rows_from(near, far, late, at, halo, ~odd, has_south)

    def read(slot):
        return [stage[slot, pl.ds(i, 8, stride=chunk)] for i in range(chunk)]

    for k in kinds:
        lay(k, ROWS_AT[k], SLOTS[k][1], own[k])
    lay(7, EAST_AT, WIDE, east[0:rows])
    lay(8, WEST_AT, WIDE, west[0:rows])
    east_parts = read(7)
    west_parts = read(8)
    ids = lane_ids(8)
    fields = []
    for k in kinds:
        at, width = SLOTS[k]
        in_east = run(ids, at, width, has_east)
        in_west = run(ids, at - width, width, has_west)
        parts = []
        for main, e, w in zip(read(k), east_parts, west_parts):
            side = jnp.where(in_east, e, jnp.where(in_west, w, 0.0))
            side = pltpu.roll(side, LANES - at, 1) if at else side
            parts.append(jnp.concatenate([main, side], axis=1)[None])
        fields.append(jnp.concatenate(parts, axis=0))
    return fields


def from_left(field):
    return pltpu.roll(field, 1, 2)


def from_right(field):
    return pltpu.roll(field, field.shape[2] - 1, 2)


def from_above(field):
    return jnp.concatenate([pltpu.roll(field[-1], 1, 0)[None], field[:-1]], axis=0)


def from_below(field):
    return jnp.concatenate([field[1:], pltpu.roll(field[0], 7, 0)[None]], axis=0)


def move_masks(codes, coef, masks):
    sides = {-1: from_right(codes), 0: codes, 1: from_left(codes)}
    ends = {-1: from_above(coef), 0: coef, 1: from_below(coef)}
    for k, (drow, dcol) in enumerate(MOVES):
        masks[k] = jnp.where((ends[drow] > 0.0) & (sides[dcol] == float(k)), 1.0, 0.0)


def inflow(flux, masks):
    sides = {-1: from_right(flux), 0: flux, 1: from_left(flux)}
    totals = {}
    for k, (drow, dcol) in enumerate(MOVES):
        term = masks[k] * sides[dcol]
        totals[drow] = totals[drow] + term if drow in totals else term
    return totals[0] + (from_above(totals[1]) + from_below(totals[-1]))


def speed(depth, coef):
    return coef * jnp.exp(jnp.log(jnp.abs(depth)) * (2.0 / 3.0))


KEEP = 1.0 - TIME_STEP * INFILTRATION


def depth_kernel(counts, own, east, west, near, far, coarse, sums, zc, uc, stage, masks, cst):
    flags = inside(counts)
    depth, rain, coef, codes = gather_fields((0, 1, 2, 3), WIDE, own, east, west, near, far, None, flags, stage)
    move_masks(codes, coef, masks)

    crows, ccols = zc.shape[0], LANES // 4
    fine = lax.broadcasted_iota(jnp.int32, (2 * LANES, LANES), 0)
    cell = lax.broadcasted_iota(jnp.int32, (2 * LANES, LANES), 1)
    place = lax.shift_right_logical(fine, 2)
    hit = ((fine < LANES + 8) & (place == cell)) | ((fine >= 2 * LANES - 8) & (place - (2 * LANES // 4 - 2) == cell - (LANES - 2)))
    pick = jnp.where(hit, 1.0, 0.0)
    has_north, has_south, has_east, has_west = flags
    rows = own.shape[1]
    odd = lax.axis_index("gy") % 2 == 1
    for k, middle in enumerate((coarse[...], east[rows : rows + crows], west[rows : rows + crows])):
        at = COARSE_AT + 2 * k
        cst[k] = jnp.zeros((16, LANES), F32)
        cst[k, 1:3] = rows_from(near, far, None, at, 2, odd, has_north)
        cst[k, 3 : 3 + crows] = middle
        cst[k, 3 + crows : 5 + crows] = rows_from(near, far, None, at, 2, ~odd, has_south)
    ids = lane_ids(16)
    e_here = (ids >= ccols) & (ids < jnp.where(has_east, ccols + 2, ccols))
    w_here = ids >= jnp.where(has_west, LANES - 2, LANES)
    pair = []
    for shift in (0, ccols):
        main = pltpu.roll(cst[0], LANES - shift, 1) if shift else cst[0]
        e = pltpu.roll(cst[1], (LANES + ccols - shift) % LANES, 1) if shift != ccols else cst[1]
        w = pltpu.roll(cst[2], (2 * LANES - ccols - shift) % LANES, 1)
        pair.append(jnp.where(ids < ccols, main, jnp.where(e_here, e, jnp.where(w_here, w, 0.0))))
    weight, pump = pair


    def step(_, carry):
        now, total = carry
        flux = speed(now, coef) * now
        return now * KEEP - flux + rain + inflow(flux, masks), total + now

    now, total = lax.fori_loop(0, SUBSTEPS - 1, step, (depth, jnp.zeros_like(depth)), unroll=True)
    total = total + now
    chunk = total.shape[0]
    for i in range(chunk):
        stage[0, pl.ds(i, 8, stride=chunk)] = total[i, :, :LANES]
        stage[1, pl.ds(i, 8, stride=chunk)] = total[i, :, LANES:]
    blocks = []
    for b in range(2):
        quads = [stage[b, pl.ds(8 + j, 16, stride=4)] for j in range(4)]
        blocks.append((quads[0] + quads[1]) + (quads[2] + quads[3]))
    pooled = jnp.concatenate(blocks, axis=1)
    rc = jnp.dot(
        pooled,
        pick,
        precision=lax.Precision.HIGHEST,
        preferred_element_type=F32,
    ) * (INFILTRATION * TIME_STEP)

    def beside(v):
        return (pltpu.roll(v, 1, 1) + pltpu.roll(v, LANES - 1, 1)) + (pltpu.roll(v, 1, 0) + pltpu.roll(v, 15, 0))

    drive = rc - pump
    z = weight * drive
    nz = beside(z)
    u = weight * nz
    nu = beside(u)
    mine = (ids < ccols)[3 : 3 + crows]
    cut = lambda v: v[3 : 3 + crows]
    z, nz, u, nu, drive = cut(z), cut(nz), cut(u), cut(nu), cut(drive)
    z = jnp.where(mine, z, 0.0)
    u = jnp.where(mine, u, 0.0)
    row = jnp.zeros((crows, LANES), F32)
    for k, (a, b) in enumerate(((drive, z), (z, nz), (u, nz), (u, nu))):
        part = a * b
        row = row + (pltpu.roll(part, k * ccols, 1) if k else part)
    row = jnp.sum(row, axis=0, keepdims=True)
    sums[...] = jnp.broadcast_to(row, sums.shape)
    zc[...] = z
    uc[...] = u


def state_kernel(counts, own, east, west, far, near, far_late, near_late, depth_out, tracers_out, stage, masks):
    flags = inside(counts)
    depth, rain, coef, codes, *species = gather_fields(
        (0, 1, 2, 3, 4, 5, 6), SLIM, own, east, west, near, far, (near_late, far_late), flags, stage
    )
    move_masks(codes, coef, masks)

    def step(_, carry):
        now = carry[0]
        rate = speed(now, coef)
        flux = rate * now
        new = [now * KEEP - flux + rain + inflow(flux, masks)]
        for held in carry[1:]:
            flux = rate * held
            new.append(held * KEEP - flux + inflow(flux, masks))
        return tuple(new)

    final = lax.fori_loop(0, SUBSTEPS, step, (depth, *species), unroll=4)
    chunk = depth.shape[0]
    rows = own.shape[1]
    for k, field in enumerate(final):
        for i in range(chunk):
            stage[k, pl.ds(i, 8, stride=chunk)] = field[i, :, :LANES]
        if k == 0:
            depth_out[...] = stage[k, SLIM : SLIM + rows]
        else:
            tracers_out[k - 1] = stage[k, SLIM : SLIM + rows]


def head_kernel(sums, zc, uc, head):
    total = jnp.sum(sums[...], axis=0, keepdims=True)
    run = LANES // 4
    ids = lane_ids(1)
    n0, n1, n2, n3 = (
        jnp.sum(jnp.where((ids >= k * run) & (ids < (k + 1) * run), total, 0.0), axis=1, keepdims=True)
        for k in range(4)
    )
    pq = n0 - n1
    a0 = n0 / pq
    ratio = (n0 * n2 - n1 * n1) / (pq * pq)
    slope = (n1 - n2) / pq
    below = (n2 - n3) - slope * (n1 - n2)
    a1 = jnp.where(below > 0.0, n0 * ratio / jnp.where(below > 0.0, below, 1.0), 0.0) / a0
    wide = head.shape[1]
    head[...] = ((a0 - a1 * slope) * zc[...] + a1 * uc[...])[:, :wide]


def swaps(axis, offset, counts):
    pairs = []
    for col in range(counts[0]):
        for row in range(counts[1]):
            spot = [col, row]
            k = AXES.index(axis)
            other = ((spot[k] + offset) ^ 1) - offset
            if 0 <= other < counts[k]:
                spot[k] = other
            else:
                spot[1 - k] ^= 1
            pairs.append((col * counts[1] + row, spot[0] * counts[1] + spot[1]))
    return pairs


def exchange(near, far, axis, counts):
    near = lax.ppermute(near, AXES, swaps(axis, 0, counts))
    far = lax.ppermute(far, AXES, swaps(axis, 1, counts))
    return near, far


def shards(counts, *inputs):
    rows, cols = inputs[0].shape
    crows, ccols = inputs[6].shape
    shape = lambda *dims: jax.ShapeDtypeStruct(dims, F32)
    own, near, far, coarse = pl.pallas_call(
        pack_columns,
        out_shape=(shape(7, rows, cols), shape(rows + crows, LANES), shape(rows + crows, LANES), shape(crows, LANES)),
        in_specs=[pl.BlockSpec(memory_space=pltpu.MemorySpace.HBM)] * 9,
        out_specs=tuple(whole(4)),
        scratch_shapes=[pltpu.VMEM(a.shape, a.dtype) for a in inputs] + [pltpu.SemaphoreType.DMA((9,))],
        compiler_params=SMALL,
        name="pack_columns",
    )(*[pltpu.with_memory_space_constraint(a, pltpu.MemorySpace.HBM) for a in inputs])
    near, far = exchange(near, far, "gx", counts)
    near, far, near_late, far_late, east, west = pl.pallas_call(
        pack_rows,
        out_shape=(
            shape(EARLY, LANES),
            shape(EARLY, LANES),
            shape(STRIP - EARLY, LANES),
            shape(STRIP - EARLY, LANES),
            shape(rows + crows, LANES),
            shape(rows + crows, LANES),
        ),
        in_specs=whole(4),
        out_specs=tuple(whole(6)),
        compiler_params=SMALL,
        name="pack_rows",
    )(own, far, near, coarse)
    near, far = exchange(near, far, "gy", counts)
    near_late, far_late = exchange(near_late, far_late, "gy", counts)
    deep = rows + 2 * WIDE
    sums, zc, uc = pl.pallas_call(
        functools.partial(depth_kernel, counts),
        out_shape=(shape(counts[0] * counts[1], LANES), shape(crows, LANES), shape(crows, LANES)),
        in_specs=whole(6),
        out_specs=tuple(whole(3)),
        scratch_shapes=[
            pltpu.VMEM((9, deep, LANES), F32),
            pltpu.VMEM((8, deep // 8, 8, 2 * LANES), F32),
            pltpu.VMEM((3, 16, LANES), F32),
        ],
        compiler_params=ROOMY,
        cost_estimate=pl.CostEstimate(flops=20000000, bytes_accessed=20000000, transcendentals=0),
        name="depth_and_moments",
    )(own, east, west, near, far, coarse)
    sums, near_late, far_late = lax.optimization_barrier((sums, near_late, far_late))
    low = rows + 2 * SLIM
    depth_out, tracers_out = pl.pallas_call(
        functools.partial(state_kernel, counts),
        out_shape=(shape(rows, cols), shape(3, rows, cols)),
        in_specs=whole(7),
        out_specs=tuple(whole(2)),
        scratch_shapes=[
            pltpu.VMEM((9, low, LANES), F32),
            pltpu.VMEM((8, low // 8, 8, 2 * LANES), F32),
        ],
        cost_estimate=pl.CostEstimate(flops=20_000_000, bytes_accessed=20_000_000, transcendentals=0),
        compiler_params=ROOMY,
        name="all_channels",
    )(own, east, west, far, near, far_late, near_late)
    sums = lax.all_to_all(sums, AXES, 0, 0, tiled=True)
    head = pl.pallas_call(
        head_kernel,
        out_shape=shape(crows, ccols),
        in_specs=whole(3),
        out_specs=pl.BlockSpec(memory_space=pltpu.VMEM),
        compiler_params=SMALL,
        name="combine_head",
    )(sums, zc, uc)
    return depth_out, tracers_out, head


def solution(mesh):
    counts = (mesh.shape["gx"], mesh.shape["gy"])
    tile = P("gy", "gx")
    deep = P(None, "gy", "gx")
    return jax.shard_map(
        functools.partial(shards, counts),
        mesh=mesh,
        in_specs=(tile, deep) + (tile,) * 7,
        out_specs=(tile, deep, tile),
        check_vma=False,
    )
```

```python
import functools

import jax
import jax.numpy as jnp
from jax import lax
from jax.experimental import pallas as pl
from jax.experimental.pallas import tpu as pltpu
from jax.sharding import PartitionSpec as P

SUBSTEPS = 12
TIME_STEP = 0.2
INFILTRATION = 0.05
MOVES = ((-1, -1), (-1, 0), (-1, 1), (0, -1), (0, 1), (1, -1), (1, 0), (1, 1))
AXES = ("gx", "gy")

WIDE = 20
SLIM = 12
LANES = 128
SLOTS = ((0, WIDE), (WIDE, WIDE), (2 * WIDE, WIDE), (3 * WIDE, WIDE)) + tuple(
    (4 * WIDE + k * SLIM, SLIM) for k in range(3)
)
EAST_AT = 4 * WIDE
WEST_AT = EAST_AT + WIDE
COARSE_AT = WEST_AT + WIDE
EARLY = 128
ROWS_AT = (0, WIDE, 2 * WIDE, 3 * WIDE) + tuple(EARLY + k * SLIM for k in range(3))
STRIP = 168
F32 = jnp.float32
SMALL = pltpu.CompilerParams(vmem_limit_bytes=2 << 20)
ROOMY = pltpu.CompilerParams(vmem_limit_bytes=6 << 20)


def whole(count):
    return [pl.BlockSpec(memory_space=pltpu.VMEM)] * count


def run(ids, start, width, present):
    start = start % LANES
    return (ids >= start) & (ids < (start + width if present is True else jnp.where(present, start + width, start)))


def lane_ids(rows):
    return lax.broadcasted_iota(jnp.int32, (rows, LANES), 1)


def pack_columns(*refs):
    sources, (own, near, far, coarse), buffers, done = refs[:9], refs[9:13], refs[13:22], refs[22]
    copies = [pltpu.make_async_copy(a, b, done.at[k]) for k, (a, b) in enumerate(zip(sources, buffers))]
    for copy in copies:
        copy.start()
    for copy in copies:
        copy.wait()
    depth, tracers, rain, rough, codes, land_mask, leak, pump, active = buffers
    land = land_mask[...].astype(F32)
    fields = [
        depth[...] * land,
        rain[...] * land * TIME_STEP,
        rough[...] * land * TIME_STEP,
        codes[...].astype(F32),
        tracers[0] * land,
        tracers[1] * land,
        tracers[2] * land,
    ]
    rows = land.shape[0]
    ids = lane_ids(rows)
    head = jnp.zeros((rows, LANES), F32)
    tail = jnp.zeros((rows, LANES), F32)
    for field, (at, width) in zip(fields, SLOTS):
        moved = pltpu.roll(field, at, 1) if at else field
        head = jnp.where(run(ids, at, width, True), moved, head)
        tail = jnp.where(run(ids, at - width, width, True), moved, tail)
    for k, field in enumerate(fields):
        own[k] = field
    act = active[...].astype(F32)
    weight = act / (act * (4.0 + leak[...]) + (1.0 - act))
    both = jnp.concatenate([weight, pump[...], jnp.zeros((act.shape[0], LANES - 2 * act.shape[1]), F32)], axis=1)
    coarse[...] = both
    odd = lax.axis_index("gx") % 2 == 1
    near[0:rows] = jnp.where(odd, head, tail)
    far[0:rows] = jnp.where(odd, tail, head)
    near[rows : rows + act.shape[0]] = both
    far[rows : rows + act.shape[0]] = both


def pack_rows(own, side_far, side_near, coarse, near, far, near_late, far_late, east, west):
    flip = lax.axis_index("gx") % 2 == 1
    east[...] = jnp.where(flip, side_far[...], side_near[...])
    west[...] = jnp.where(flip, side_near[...], side_far[...])
    rows = own.shape[1]
    crows = coarse.shape[0]
    odd = lax.axis_index("gy") % 2 == 1

    def put(at, top, bottom):
        count = top.shape[0]
        early = at < EARLY
        at = at if early else at - EARLY
        (near if early else near_late)[at : at + count] = jnp.where(odd, top, bottom)
        (far if early else far_late)[at : at + count] = jnp.where(odd, bottom, top)

    for k, at in enumerate(ROWS_AT):
        width = SLOTS[k][1]
        put(at, own[k, 0:width], own[k, rows - width : rows])
    for at, side in ((EAST_AT, east), (WEST_AT, west)):
        put(at, side[0:WIDE], side[rows - WIDE : rows])
    for k, part in enumerate((coarse, east.at[rows : rows + crows], west.at[rows : rows + crows])):
        put(COARSE_AT + 2 * k, part[0:2], part[crows - 2 : crows])
    for start, stop in ((COARSE_AT + 6, EARLY), (ROWS_AT[-1] + SLIM, STRIP)):
        rest = jnp.zeros((stop - start, LANES), F32)
        put(start, rest, rest)


def inside(counts):
    col = lax.axis_index("gx")
    row = lax.axis_index("gy")
    return row > 0, row < counts[1] - 1, col < counts[0] - 1, col > 0


def rows_from(near, far, late, start, count, use_near, present):
    if start >= EARLY:
        (near, far), start = late, start - EARLY
    got = jnp.where(use_near, near[start : start + count], far[start : start + count])
    return jnp.where(present, got, 0.0)


def gather_fields(kinds, halo, own, east, west, near, far, late, flags, stage):
    has_north, has_south, has_east, has_west = flags
    rows = own.shape[1]
    total = rows + 2 * halo
    chunk = total // 8
    odd = lax.axis_index("gy") % 2 == 1

    def lay(slot, at, width, middle):
        stage[slot, 0:halo] = rows_from(near, far, late, at + width - halo, halo, odd, has_north)
        stage[slot, halo : halo + rows] = middle
        stage[slot, halo + rows : total] = rows_from(near, far, late, at, halo, ~odd, has_south)

    def read(slot):
        return [stage[slot, pl.ds(i, 8, stride=chunk)] for i in range(chunk)]

    for k in kinds:
        lay(k, ROWS_AT[k], SLOTS[k][1], own[k])
    lay(7, EAST_AT, WIDE, east[0:rows])
    lay(8, WEST_AT, WIDE, west[0:rows])
    east_parts = read(7)
    west_parts = read(8)
    ids = lane_ids(8)
    fields = []
    for k in kinds:
        at, width = SLOTS[k]
        in_east = run(ids, at, width, has_east)
        in_west = run(ids, at - width, width, has_west)
        parts = []
        for main, e, w in zip(read(k), east_parts, west_parts):
            side = jnp.where(in_east, e, jnp.where(in_west, w, 0.0))
            side = pltpu.roll(side, LANES - at, 1) if at else side
            parts.append(jnp.concatenate([main, side], axis=1)[None])
        fields.append(jnp.concatenate(parts, axis=0))
    return fields


def from_left(field):
    return pltpu.roll(field, 1, 2)


def from_right(field):
    return pltpu.roll(field, field.shape[2] - 1, 2)


def from_above(field):
    return jnp.concatenate([pltpu.roll(field[-1], 1, 0)[None], field[:-1]], axis=0)


def from_below(field):
    return jnp.concatenate([field[1:], pltpu.roll(field[0], 7, 0)[None]], axis=0)


def move_masks(codes, coef, masks):
    sides = {-1: from_right(codes), 0: codes, 1: from_left(codes)}
    ends = {-1: from_above(coef), 0: coef, 1: from_below(coef)}
    for k, (drow, dcol) in enumerate(MOVES):
        masks[k] = jnp.where((ends[drow] > 0.0) & (sides[dcol] == float(k)), 1.0, 0.0)


def inflow(flux, masks):
    sides = {-1: from_right(flux), 0: flux, 1: from_left(flux)}
    totals = {}
    for k, (drow, dcol) in enumerate(MOVES):
        term = masks[k] * sides[dcol]
        totals[drow] = totals[drow] + term if drow in totals else term
    return totals[0] + (from_above(totals[1]) + from_below(totals[-1]))


def speed(depth, coef):
    return coef * jnp.exp(jnp.log(jnp.abs(depth)) * (2.0 / 3.0))


KEEP = 1.0 - TIME_STEP * INFILTRATION


def depth_kernel(counts, own, east, west, far, near, coarse, sums, zc, uc, stage, masks, cst):
    flags = inside(counts)
    depth, rain, coef, codes = gather_fields((0, 1, 2, 3), WIDE, own, east, west, near, far, None, flags, stage)
    move_masks(codes, coef, masks)

    crows, ccols = zc.shape[0], LANES // 4
    fine = lax.broadcasted_iota(jnp.int32, (2 * LANES, LANES), 0)
    cell = lax.broadcasted_iota(jnp.int32, (2 * LANES, LANES), 1)
    place = lax.shift_right_logical(fine, 2)
    hit = ((fine < LANES + 8) & (place == cell)) | ((fine >= 2 * LANES - 8) & (place - (2 * LANES // 4 - 2) == cell - (LANES - 2)))
    pick = jnp.where(hit, 1.0, 0.0)
    has_north, has_south, has_east, has_west = flags
    rows = own.shape[1]
    odd = lax.axis_index("gy") % 2 == 1
    for k, middle in enumerate((coarse[...], east[rows : rows + crows], west[rows : rows + crows])):
        at = COARSE_AT + 2 * k
        cst[k] = jnp.zeros((16, LANES), F32)
        cst[k, 1:3] = rows_from(near, far, None, at, 2, odd, has_north)
        cst[k, 3 : 3 + crows] = middle
        cst[k, 3 + crows : 5 + crows] = rows_from(near, far, None, at, 2, ~odd, has_south)
    ids = lane_ids(16)
    e_here = (ids >= ccols) & (ids < jnp.where(has_east, ccols + 2, ccols))
    w_here = ids >= jnp.where(has_west, LANES - 2, LANES)
    pair = []
    for shift in (0, ccols):
        main = pltpu.roll(cst[0], LANES - shift, 1) if shift else cst[0]
        e = pltpu.roll(cst[1], (LANES + ccols - shift) % LANES, 1) if shift != ccols else cst[1]
        w = pltpu.roll(cst[2], (2 * LANES - ccols - shift) % LANES, 1)
        pair.append(jnp.where(ids < ccols, main, jnp.where(e_here, e, jnp.where(w_here, w, 0.0))))
    weight, pump = pair


    def step(_, carry):
        now, total = carry
        flux = speed(now, coef) * now
        return now * KEEP - flux + rain + inflow(flux, masks), total + now

    now, total = lax.fori_loop(0, SUBSTEPS - 1, step, (depth, jnp.zeros_like(depth)), unroll=True)
    total = total + now
    chunk = total.shape[0]
    for i in range(chunk):
        stage[0, pl.ds(i, 8, stride=chunk)] = total[i, :, :LANES]
        stage[1, pl.ds(i, 8, stride=chunk)] = total[i, :, LANES:]
    blocks = []
    for b in range(2):
        quads = [stage[b, pl.ds(8 + j, 16, stride=4)] for j in range(4)]
        blocks.append((quads[0] + quads[1]) + (quads[2] + quads[3]))
    pooled = jnp.concatenate(blocks, axis=1)
    rc = jnp.dot(
        pooled,
        pick,
        precision=lax.Precision.HIGHEST,
        preferred_element_type=F32,
    ) * (INFILTRATION * TIME_STEP)

    def beside(v):
        return (pltpu.roll(v, 1, 1) + pltpu.roll(v, LANES - 1, 1)) + (pltpu.roll(v, 1, 0) + pltpu.roll(v, 15, 0))

    drive = rc - pump
    z = weight * drive
    nz = beside(z)
    u = weight * nz
    nu = beside(u)
    mine = (ids < ccols)[3 : 3 + crows]
    cut = lambda v: v[3 : 3 + crows]
    z, nz, u, nu, drive = cut(z), cut(nz), cut(u), cut(nu), cut(drive)
    z = jnp.where(mine, z, 0.0)
    u = jnp.where(mine, u, 0.0)
    row = jnp.zeros((crows, LANES), F32)
    for k, (a, b) in enumerate(((drive, z), (z, nz), (u, nz), (u, nu))):
        part = a * b
        row = row + (pltpu.roll(part, k * ccols, 1) if k else part)
    row = jnp.sum(row, axis=0, keepdims=True)
    sums[...] = jnp.broadcast_to(row, sums.shape)
    zc[...] = z
    uc[...] = u


def state_kernel(counts, own, east, west, far, near, far_late, near_late, depth_out, tracers_out, stage, masks):
    flags = inside(counts)
    depth, rain, coef, codes, *species = gather_fields(
        (0, 1, 2, 3, 4, 5, 6), SLIM, own, east, west, near, far, (near_late, far_late), flags, stage
    )
    move_masks(codes, coef, masks)

    def step(_, carry):
        now = carry[0]
        rate = speed(now, coef)
        flux = rate * now
        new = [now * KEEP - flux + rain + inflow(flux, masks)]
        for held in carry[1:]:
            flux = rate * held
            new.append(held * KEEP - flux + inflow(flux, masks))
        return tuple(new)

    final = lax.fori_loop(0, SUBSTEPS, step, (depth, *species), unroll=True)
    chunk = depth.shape[0]
    rows = own.shape[1]
    for k, field in enumerate(final):
        for i in range(chunk):
            stage[k, pl.ds(i, 8, stride=chunk)] = field[i, :, :LANES]
        if k == 0:
            depth_out[...] = stage[k, SLIM : SLIM + rows]
        else:
            tracers_out[k - 1] = stage[k, SLIM : SLIM + rows]


def head_kernel(sums, zc, uc, head):
    total = jnp.sum(sums[...], axis=0, keepdims=True)
    run = LANES // 4
    ids = lane_ids(1)
    n0, n1, n2, n3 = (
        jnp.sum(jnp.where((ids >= k * run) & (ids < (k + 1) * run), total, 0.0), axis=1, keepdims=True)
        for k in range(4)
    )
    pq = n0 - n1
    a0 = n0 / pq
    ratio = (n0 * n2 - n1 * n1) / (pq * pq)
    slope = (n1 - n2) / pq
    below = (n2 - n3) - slope * (n1 - n2)
    a1 = jnp.where(below > 0.0, n0 * ratio / jnp.where(below > 0.0, below, 1.0), 0.0) / a0
    wide = head.shape[1]
    head[...] = ((a0 - a1 * slope) * zc[...] + a1 * uc[...])[:, :wide]


def swaps(axis, offset, counts):
    pairs = []
    for col in range(counts[0]):
        for row in range(counts[1]):
            spot = [col, row]
            k = AXES.index(axis)
            other = ((spot[k] + offset) ^ 1) - offset
            if 0 <= other < counts[k]:
                spot[k] = other
            else:
                spot[1 - k] ^= 1
            pairs.append((col * counts[1] + row, spot[0] * counts[1] + spot[1]))
    return pairs


def exchange(near, far, axis, counts):
    near = lax.ppermute(near, AXES, swaps(axis, 0, counts))
    far = lax.ppermute(far, AXES, swaps(axis, 1, counts))
    return near, far


def shards(counts, *inputs):
    rows, cols = inputs[0].shape
    crows, ccols = inputs[6].shape
    shape = lambda *dims: jax.ShapeDtypeStruct(dims, F32)
    own, near, far, coarse = pl.pallas_call(
        pack_columns,
        out_shape=(shape(7, rows, cols), shape(rows + crows, LANES), shape(rows + crows, LANES), shape(crows, LANES)),
        in_specs=[pl.BlockSpec(memory_space=pltpu.MemorySpace.HBM)] * 9,
        out_specs=tuple(whole(4)),
        scratch_shapes=[pltpu.VMEM(a.shape, a.dtype) for a in inputs] + [pltpu.SemaphoreType.DMA((9,))],
        compiler_params=SMALL,
        name="pack_columns",
    )(*[pltpu.with_memory_space_constraint(a, pltpu.MemorySpace.HBM) for a in inputs])
    near, far = exchange(near, far, "gx", counts)
    near, far, near_late, far_late, east, west = pl.pallas_call(
        pack_rows,
        out_shape=(
            shape(EARLY, LANES),
            shape(EARLY, LANES),
            shape(STRIP - EARLY, LANES),
            shape(STRIP - EARLY, LANES),
            shape(rows + crows, LANES),
            shape(rows + crows, LANES),
        ),
        in_specs=whole(4),
        out_specs=tuple(whole(6)),
        compiler_params=SMALL,
        name="pack_rows",
    )(own, far, near, coarse)
    near, far = exchange(near, far, "gy", counts)
    near_late, far_late = exchange(near_late, far_late, "gy", counts)
    deep = rows + 2 * WIDE
    sums, zc, uc = pl.pallas_call(
        functools.partial(depth_kernel, counts),
        out_shape=(shape(counts[0] * counts[1], LANES), shape(crows, LANES), shape(crows, LANES)),
        in_specs=whole(6),
        out_specs=tuple(whole(3)),
        scratch_shapes=[
            pltpu.VMEM((9, deep, LANES), F32),
            pltpu.VMEM((8, deep // 8, 8, 2 * LANES), F32),
            pltpu.VMEM((3, 16, LANES), F32),
        ],
        compiler_params=ROOMY,
        cost_estimate=pl.CostEstimate(flops=20000000, bytes_accessed=20000000, transcendentals=0),
        name="depth_and_moments",
    )(own, east, west, far, near, coarse)
    sums, near_late, far_late = lax.optimization_barrier((sums, near_late, far_late))
    low = rows + 2 * SLIM
    depth_out, tracers_out = pl.pallas_call(
        functools.partial(state_kernel, counts),
        out_shape=(shape(rows, cols), shape(3, rows, cols)),
        in_specs=whole(7),
        out_specs=tuple(whole(2)),
        scratch_shapes=[
            pltpu.VMEM((9, low, LANES), F32),
            pltpu.VMEM((8, low // 8, 8, 2 * LANES), F32),
        ],
        cost_estimate=pl.CostEstimate(flops=20_000_000, bytes_accessed=20_000_000, transcendentals=0),
        compiler_params=ROOMY,
        name="all_channels",
    )(own, east, west, far, near, far_late, near_late)
    sums = lax.all_to_all(sums, AXES, 0, 0, tiled=True)
    head = pl.pallas_call(
        head_kernel,
        out_shape=shape(crows, ccols),
        in_specs=whole(3),
        out_specs=pl.BlockSpec(memory_space=pltpu.VMEM),
        compiler_params=SMALL,
        name="combine_head",
    )(sums, zc, uc)
    return depth_out, tracers_out, head


def solution(mesh):
    counts = (mesh.shape["gx"], mesh.shape["gy"])
    tile = P("gy", "gx")
    deep = P(None, "gy", "gx")
    return jax.shard_map(
        functools.partial(shards, counts),
        mesh=mesh,
        in_specs=(tile, deep) + (tile,) * 7,
        out_specs=(tile, deep, tile),
        check_vma=False,
    )
```
